512 devices in a mesh: seq: 16 (over x, z_lo, core), head: 32 (over z_hi, y).
Axes of the slice: x: 4, y: 8, z: 8 (z_hi: 4, z_lo: 2; z = z_hi * 2 + z_lo), core: 2. Of those that a mesh axis runs over, the one named last changes fastest.
Arguments:
- query_heads: bfloat16 [8192, 16, 128], P(('seq', 'head')), may hold values from -6 to 6
- key_heads: bfloat16 [8192, 16, 128], P(('seq', 'head')), may hold values from -6 to 6
- value_heads: bfloat16 [8192, 32, 128], P(('seq', 'head')), may hold values from -6 to 6
- gate_log: bfloat16 [8192, 32], P(('seq', 'head')), may hold values from -1 to 0
- beta_rate: bfloat16 [8192, 32], P(('seq', 'head')), may hold values from 0.0099487305 to 0.099609375
Outputs:
- head_output: bfloat16 [8192, 4096], P(('seq', 'head'))
- block_states: float32 [16, 32, 128, 128], P('seq', 'head')
The draws below stay inside these ranges and needn't reach their ends.
All inputs are finite; a program needn't handle non-finite values.
Results may differ from the reference program's by a relative error of at most 0.001.
Values may be sent and summed in bfloat16 or wider, within the bound.
No kernel may reach another device: no remote copies, remote signals or barrier semaphores. Data moves between devices by JAX's collectives and lax.ppermute only.
A program may use at most 64 MiB of HBM per device.

```python
import jax
import jax.numpy as jnp
from jax import lax

VALUE_HEAD_COUNT = 32
HK = 16
DK = 128
DV = 128
STRETCH = 64
SLAB = 512
PROMPT_TOKENS = 8192
N_SEQ = 16


def draw_gate_log(key, part):
    random_subkeys = jax.random.split(key, 7)
    fast_share = 0.5
    fast_head = jax.random.uniform(random_subkeys[0], (VALUE_HEAD_COUNT,)) < fast_share
    fast_rate = jnp.exp(jax.random.uniform(random_subkeys[1], (VALUE_HEAD_COUNT,), minval=jnp.log(1.0 / 50.0), maxval=jnp.log(1.0 / 30.0)))
    slow_rate = jax.random.uniform(random_subkeys[2], (VALUE_HEAD_COUNT,), minval=0.2, maxval=0.8) / PROMPT_TOKENS
    base_rate = jnp.where(fast_head, fast_rate, slow_rate)
    slab_factor = jnp.exp(jax.random.uniform(random_subkeys[3], (PROMPT_TOKENS // SLAB, 1, VALUE_HEAD_COUNT), minval=-0.7, maxval=0.7))
    token_factor = jnp.exp(jax.random.uniform(random_subkeys[4], (PROMPT_TOKENS // SLAB, SLAB, VALUE_HEAD_COUNT), minval=-0.5, maxval=0.5))
    decay_factor = (base_rate * slab_factor * token_factor).reshape(PROMPT_TOKENS, VALUE_HEAD_COUNT)
    doubling_reached = jax.random.uniform(random_subkeys[5], (PROMPT_TOKENS, VALUE_HEAD_COUNT)) < 2.0 / PROMPT_TOKENS
    doubling_depth = jax.random.uniform(random_subkeys[6], (PROMPT_TOKENS, VALUE_HEAD_COUNT), minval=jnp.log(0.5), maxval=jnp.log(0.8))
    return (jnp.where(doubling_reached, doubling_depth, 0.0) - decay_factor).astype(jnp.bfloat16)


def shard_levels(key, shape, cuts, low, top_value):
    level = 1.0
    for position, parts in cuts:
        heights = jax.random.uniform(jax.random.fold_in(jax.random.fold_in(key, 6), position), (parts,), jnp.float32, low / len(cuts), top_value / len(cuts))
        level = level * jnp.repeat(jnp.exp(heights), shape[position] // parts).reshape((-1,) + (1,) * (len(shape) - 1 - position))
    return level


def normal_values(stream_key, shape, deviation, limit, cuts=(), kind=jnp.bfloat16):
    array = jax.random.normal(stream_key, shape, jnp.float32) * deviation
    if len(cuts) > 0:
        array = shard_levels(stream_key, shape, cuts, -0.22, 0.18) * array
    return jnp.clip(array, min=-limit, max=limit).astype(kind)


def setup_inputs(seed: int = 0) -> dict:
    key_of = jax.random.split(jax.random.key(seed), 6)
    query_heads = normal_values(key_of[0], (PROMPT_TOKENS, HK, DK), 1.0, 6.0, ((0, 512),))
    key_heads = normal_values(key_of[1], (PROMPT_TOKENS, HK, DK), 1.0, 6.0, ((0, 512),))
    value_heads = normal_values(key_of[2], (PROMPT_TOKENS, VALUE_HEAD_COUNT, DV), 1.0, 6.0, ((0, 512),))
    gate_log = draw_gate_log(jax.random.fold_in(key_of[5], 71), 0)
    beta_rate = jnp.clip(0.0099487305 + 0.089660645 * jax.random.uniform(key_of[4], (PROMPT_TOKENS, VALUE_HEAD_COUNT), jnp.float32) ** shard_levels(key_of[4], (PROMPT_TOKENS, VALUE_HEAD_COUNT), ((0, 512),), -0.2, 0.2), 0.0099487305, 0.099609375).astype(jnp.bfloat16)
    return {"query_heads": query_heads, "key_heads": key_heads, "value_heads": value_heads, "gate_log": gate_log, "beta_rate": beta_rate}


HIGHEST = lax.Precision.HIGHEST

def normalize(tensor):
    tensor = tensor.astype(jnp.float32)
    return tensor / jnp.sqrt(lax.optimization_barrier(jnp.sum(tensor * tensor, axis=-1, keepdims=True)) + 1e-06)

def stretch_parts(queries, keys_in, values, gate_vals, beta_vals):
    span_len = gate_vals.shape[-1]
    cumulative = jnp.cumsum(gate_vals, axis=-1)
    row_ids = lax.broadcasted_iota(jnp.int32, (span_len, span_len), 0)
    columns = lax.broadcasted_iota(jnp.int32, (span_len, span_len), 1)
    strict = row_ids > columns
    inclusive = row_ids >= columns
    differ = cumulative[..., :, None] - cumulative[..., None, :]
    key_key = jnp.einsum('...rd,...sd->...rs', keys_in, keys_in, precision=HIGHEST)
    query_key = jnp.einsum('...rd,...sd->...rs', queries, keys_in, precision=HIGHEST)
    lower_triangle = jnp.where(strict, beta_vals[..., :, None] * jnp.exp(jnp.where(strict, differ, 0.0)) * key_key, 0.0)
    scores = jnp.where(inclusive, jnp.exp(jnp.where(inclusive, differ, 0.0)) * query_key, 0.0)
    identity = jnp.eye(span_len, dtype=jnp.float32)
    right_side = jnp.concatenate([(beta_vals * jnp.exp(cumulative))[..., None] * keys_in, beta_vals[..., None] * values], axis=-1)
    solved = jax.scipy.linalg.solve_triangular(identity + lower_triangle, right_side, lower=True, unit_diagonal=True)
    key_width = keys_in.shape[-1]
    last_cum = cumulative[..., -1:]
    query_dec = jnp.exp(cumulative)[..., None] * queries
    key_dec = jnp.exp(last_cum - cumulative)[..., None] * keys_in
    return (solved[..., :key_width], solved[..., key_width:], scores, query_dec, key_dec, jnp.exp(last_cum[..., 0]))

def stretch_step(carried, pieces):
    query_part, key_segment, value_part, gate_part, beta_part = pieces
    grouping = value_part.shape[1] // query_part.shape[1]
    queries = jnp.swapaxes(jnp.repeat(normalize(query_part), grouping, axis=1), 0, 1)
    keys_in = jnp.swapaxes(jnp.repeat(normalize(key_segment), grouping, axis=1), 0, 1)
    values = jnp.swapaxes(value_part.astype(jnp.float32), 0, 1)
    gate_vals = jnp.swapaxes(gate_part.astype(jnp.float32), 0, 1)
    beta_vals = jnp.swapaxes(beta_part.astype(jnp.float32), 0, 1)
    write_keys, write_vals, scores, query_dec, key_dec, stretch_decay = stretch_parts(queries, keys_in, values, gate_vals, beta_vals)
    fresh_vals = write_vals - jnp.einsum('hcd,hde->hce', write_keys, carried, precision=HIGHEST)
    outputs = jnp.einsum('hcd,hde->hce', query_dec, carried, precision=HIGHEST) + jnp.einsum('hrs,hse->hre', scores, fresh_vals, precision=HIGHEST)
    carried = stretch_decay[:, None, None] * carried + jnp.einsum('hcd,hce->hde', key_dec, fresh_vals, precision=HIGHEST)
    return (carried, jnp.swapaxes(outputs, 0, 1).astype(jnp.bfloat16))

def reference(query_heads, key_heads, value_heads, gate_log, beta_rate):
    blocks = SLAB // STRETCH

    def arrange(tensor):
        return tensor.reshape((N_SEQ, blocks, STRETCH) + tensor.shape[1:])

    def slab_step(carried, pieces):
        carried, outputs = lax.scan(stretch_step, carried, pieces)
        return (carried, (carried, outputs))
    initial = jnp.zeros((VALUE_HEAD_COUNT, DK, DV), jnp.float32)
    last_state, (block_states, outputs) = lax.scan(slab_step, initial, (arrange(query_heads), arrange(key_heads), arrange(value_heads), arrange(gate_log), arrange(beta_rate)))
    return (outputs.reshape(PROMPT_TOKENS, VALUE_HEAD_COUNT * DV), block_states)
```

```python
import jax
import jax.numpy as jnp
from jax import lax
from jax.experimental import pallas as pl
from jax.experimental.pallas import tpu as pltpu
from jax.sharding import PartitionSpec as P

F32 = jnp.float32
BF16 = jnp.bfloat16
TOK = 512
DIM = 128
SRC = 32
PER = 16
HALF = 256


def iota(shape, dim):
    return lax.broadcasted_iota(jnp.int32, shape, dim)


def dot1(a, b):
    return lax.dot_general(a, b, (((1,), (0,)), ((), ())), preferred_element_type=F32)


def dot_t(a, b):
    return lax.dot_general(a, b, (((1,), (1,)), ((), ())), preferred_element_type=F32)


def split(a):
    high = a.astype(BF16)
    return high, (a - high.astype(F32)).astype(BF16)


def dot3(a, b):
    ah, al = split(a)
    bh, bl = split(b)
    return dot1(ah, bh) + (dot1(ah, bl) + dot1(al, bh))


def inv_norm(total):
    total = total + 1e-6
    y = lax.rsqrt(total)
    return y * (1.5 - 0.5 * total * y * y)


def row_sums(x):
    squares = x.astype(F32) * x.astype(F32)
    column = jnp.sum(squares, axis=1, keepdims=True)
    high, low = split(squares)
    ones = jnp.ones((8, DIM), BF16)
    row = (dot_t(ones, high) + dot_t(ones, low))[0:1]
    return column, row


def columns_of(got_ref):
    extra = got_ref[:, 48:56, :].astype(F32)
    lanes = extra[:, 0, :].astype(BF16)
    spread = (iota((TOK, SRC), 0) // PER == iota((TOK, SRC), 1)).astype(F32).astype(BF16)
    rows = dot1(spread, lanes)
    lane = iota((TOK, DIM), 1)
    spot = iota((TOK, DIM), 0) % PER
    gate = jnp.sum(jnp.where(lane == spot, rows, 0.0), axis=1, keepdims=True)
    beta = jnp.sum(jnp.where(lane == spot + PER, rows, 0.0), axis=1, keepdims=True)
    return gate, beta


def spans(gate):
    row, col = iota((TOK, TOK), 0), iota((TOK, TOK), 1)
    upto = (row >= col).astype(F32).astype(BF16)
    after = jnp.where(row > col, gate, 0.0).astype(BF16)
    return dot1(upto, after), row, col, upto


def local_kernel(got_ref, pair_ref, solved_ref):
    gate, beta = columns_of(got_ref)
    keys = got_ref[:, 16:32, :].reshape(TOK, DIM)
    values = got_ref[:, 32:48, :].reshape(TOK, DIM)
    differ, row, col, upto = spans(gate)
    k_col, k_row = row_sums(keys)
    inv_col, inv_row = inv_norm(k_col), inv_norm(k_row)
    key_key = dot_t(keys, keys)
    strict = row > col
    lower = jnp.where(
        strict, (beta * inv_col) * jnp.exp(jnp.where(strict, differ, 0.0)) * key_key * inv_row, 0.0
    )
    gate_wide = jnp.broadcast_to(gate, (TOK, DIM)).astype(BF16)
    cumul = dot1(upto, gate_wide)
    tail = jnp.sum(gate_wide.astype(F32), axis=0, keepdims=True)
    beyond = dot1((row < col).astype(F32).astype(BF16), gate_wide)
    right = jnp.concatenate(
        [
            (beta * inv_col) * jnp.exp(cumul) * keys.astype(F32),
            beta * values.astype(F32),
        ],
        axis=1,
    )
    r, c = iota((HALF, HALF), 0), iota((HALF, HALF), 1)
    inverses = []
    for part in range(2):
        block = lower[part * HALF : (part + 1) * HALF, part * HALF : (part + 1) * HALF]
        eye = jnp.where(r == c, 1.0, 0.0)
        n1 = jnp.where(r // 16 == c // 16, -block, 0.0)
        n2 = dot3(n1, n1)
        x = eye + n1 + n2 + dot3(n1, n2)
        n4 = dot3(n2, n2)
        x = x + dot3(x, n4)
        n8 = dot3(n4, n4)
        x = x + dot3(x, n8)
        for width in (16, 32, 64, 128):
            here = (r // (2 * width) == c // (2 * width)) & (r // width != c // width)
            x = x - dot3(x, dot3(jnp.where(here, block, 0.0), x))
        inverses.append(x)
    top = dot3(inverses[0], right[:HALF])
    bottom = dot3(inverses[1], right[HALF:] - dot3(lower[HALF:, :HALF], top))
    solved = jnp.concatenate([top, bottom], axis=0)
    solved_ref[...] = solved
    weight = inv_col * jnp.exp(beyond)
    scaled = jnp.concatenate([weight, weight], axis=1) * solved
    high, low = split(scaled)
    keys_t = keys.T
    moved = dot1(keys_t, high) + dot1(keys_t, low)
    d_row, d_col = iota((DIM, DIM), 0), iota((DIM, DIM), 1)
    carry = jnp.where(d_row == d_col, jnp.exp(tail), 0.0)
    pair_ref[:, :DIM] = carry - moved[:, :DIM]
    pair_ref[:, DIM:] = moved[:, DIM:]


def readout_kernel(got_ref, solved_ref, direct_ref, reach_ref):
    gate, _ = columns_of(got_ref)
    queries = got_ref[:, 0:16, :].reshape(TOK, DIM)
    keys = got_ref[:, 16:32, :].reshape(TOK, DIM)
    differ, row, col, upto = spans(gate)
    q_col, _ = row_sums(queries)
    _, k_row = row_sums(keys)
    query_inv = inv_norm(q_col)
    inclusive = row >= col
    scores = jnp.where(
        inclusive,
        query_inv * jnp.exp(jnp.where(inclusive, differ, 0.0)) * dot_t(queries, keys) * inv_norm(k_row),
        0.0,
    )
    cumul = dot1(upto, jnp.broadcast_to(gate, (TOK, DIM)).astype(BF16))
    solved = solved_ref[...]
    top = dot3(scores[:HALF, :HALF], solved[:HALF])
    bottom = dot3(scores[HALF:, :], solved)
    mixed = jnp.concatenate([top, bottom], axis=0)
    direct_ref[...] = mixed[:, DIM:]
    reach_ref[...] = query_inv * jnp.exp(cumul) * queries.astype(F32) - mixed[:, :DIM]


def first_kernel(own_ref, one_ref, two_ref, three_ref, before_ref, window_ref):
    later = one_ref[...]
    for ref in (two_ref, three_ref):
        step = dot3(later[:, :DIM], ref[...])
        later = jnp.concatenate([step[:, :DIM], step[:, DIM:] + later[:, DIM:]], axis=1)
    before_ref[...] = later
    step = dot3(own_ref[:, :DIM], later)
    window_ref[:, :DIM] = step[:, :DIM]
    window_ref[:, DIM:] = step[:, DIM:] + own_ref[:, DIM:]


def second_kernel(before_ref, window_ref, far_ref, before_out, state_out):
    step = dot3(before_ref[:, :DIM], far_ref[...])
    before_out[:, :DIM] = step[:, :DIM]
    before_out[:, DIM:] = step[:, DIM:] + before_ref[:, DIM:]
    state_out[...] = dot3(window_ref[:, :DIM], far_ref[:, DIM:]) + window_ref[:, DIM:]


def last_kernel(own_ref, before_ref, far_ref, direct_ref, reach_ref, out_ref, state_ref):
    incoming = dot3(before_ref[:, :DIM], far_ref[...]) + before_ref[:, DIM:]
    combined = direct_ref[...] + dot3(reach_ref[...], incoming)
    out_ref[...] = combined.astype(BF16)
    state_ref[...] = dot3(own_ref[:, :DIM], incoming) + own_ref[:, DIM:]


def call(kernel, *shapes):
    def run(*operands):
        vmem = pl.BlockSpec(memory_space=pltpu.VMEM)
        outs = tuple(jax.ShapeDtypeStruct(shape, dtype) for shape, dtype in shapes)
        return pl.pallas_call(
            kernel,
            out_shape=outs,
            in_specs=[vmem] * len(operands),
            out_specs=tuple([vmem] * len(outs)),
            compiler_params=pltpu.CompilerParams(vmem_limit_bytes=48 << 20),
        )(*operands)

    return run


def shifted(block, distance):
    count = lax.axis_size("seq")
    return lax.ppermute(block, "seq", [(i - distance, i) for i in range(distance, count)])


def per_device(query_heads, key_heads, value_heads, gate_log, beta_rate):
    grouping = value_heads.shape[1] // query_heads.shape[1]
    queries = jnp.repeat(jnp.swapaxes(query_heads, 0, 1), grouping, axis=0)
    keys = jnp.repeat(jnp.swapaxes(key_heads, 0, 1), grouping, axis=0)
    values = jnp.swapaxes(value_heads, 0, 1)
    rates = jnp.concatenate([gate_log.T, beta_rate.T], axis=1)[:, None, :]
    rates = jnp.pad(rates, ((0, 0), (0, 7), (0, DIM - 2 * PER)))
    packed = jnp.concatenate([queries, keys, values, rates], axis=1)
    got = lax.all_to_all(packed, "head", split_axis=0, concat_axis=0, tiled=True)
    pair = ((DIM, 2 * DIM), F32)
    own, solved = call(local_kernel, pair, ((TOK, 2 * DIM), F32))(got)
    near = [shifted(own, distance) for distance in (1, 2, 3)]
    direct, reach = call(readout_kernel, ((TOK, DIM), F32), ((TOK, DIM), F32))(got, solved)
    before, window = call(first_kernel, pair, pair)(own, *near)
    before, state = call(second_kernel, pair, ((DIM, DIM), F32))(before, window, shifted(window, 4))
    rows, last_state = call(last_kernel, ((TOK, DIM), BF16), ((DIM, DIM), F32))(
        own, before, shifted(state, 8), direct, reach
    )
    head_output = lax.all_to_all(rows, "head", split_axis=0, concat_axis=1, tiled=True)
    return head_output, last_state[None, None]


def solution(mesh):
    return jax.shard_map(
        per_device,
        mesh=mesh,
        in_specs=(
            P(("seq", "head"), None, None),
            P(("seq", "head"), None, None),
            P(("seq", "head"), None, None),
            P(("seq", "head"), None),
            P(("seq", "head"), None),
        ),
        out_specs=(P(("seq", "head"), None), P("seq", "head", None, None)),
        check_vma=False,
    )
```

```python
import jax
import jax.numpy as jnp
from jax import lax
from jax.experimental import pallas as pl
from jax.experimental.pallas import tpu as pltpu
from jax.sharding import PartitionSpec as P

F32 = jnp.float32
BF16 = jnp.bfloat16
TOK = 512
DIM = 128
SRC = 32
PER = 16
HALF = 256


def iota(shape, dim):
    return lax.broadcasted_iota(jnp.int32, shape, dim)


def dot1(a, b):
    return lax.dot_general(a, b, (((1,), (0,)), ((), ())), preferred_element_type=F32)


def dot_t(a, b):
    return lax.dot_general(a, b, (((1,), (1,)), ((), ())), preferred_element_type=F32)


def split(a):
    high = a.astype(BF16)
    return high, (a - high.astype(F32)).astype(BF16)


def dot3(a, b):
    ah, al = split(a)
    bh, bl = split(b)
    return dot1(ah, bh) + (dot1(ah, bl) + dot1(al, bh))


def inv_norm(total):
    total = total + 1e-6
    y = lax.rsqrt(total)
    return y * (1.5 - 0.5 * total * y * y)


def row_sums(x):
    squares = x.astype(F32) * x.astype(F32)
    column = jnp.sum(squares, axis=1, keepdims=True)
    high, low = split(squares)
    ones = jnp.ones((8, DIM), BF16)
    row = (dot_t(ones, high) + dot_t(ones, low))[0:1]
    return column, row


def dot_pair(a, b):
    ah, al = split(a)
    bh, bl = split(b)
    return dot1(jnp.concatenate([ah, al], axis=1), jnp.concatenate([bh, bh], axis=0)) + dot1(ah, bl)


def columns_of(got_ref):
    lanes = got_ref[:, 48:56, :].astype(F32)[:, 0, :].astype(BF16)
    token, source = iota((TOK, SRC), 0), iota((TOK, SRC), 1)
    spread = ((token >> 4) == source).astype(F32).astype(BF16)
    rows = dot1(spread, lanes)
    lane = iota((TOK, DIM), 1)
    spot = iota((TOK, DIM), 0) & (PER - 1)
    gate = jnp.sum(jnp.where(lane == spot, rows, 0.0), axis=1, keepdims=True)
    beta = jnp.sum(jnp.where(lane == spot + PER, rows, 0.0), axis=1, keepdims=True)
    return gate, beta


def spans(gate):
    row, col = iota((HALF, HALF), 0), iota((HALF, HALF), 1)
    upto = (row >= col).astype(F32).astype(BF16)
    first, second = gate[:HALF], gate[HALF:]
    after1 = jnp.where(row > col, first, 0.0).astype(BF16)
    after2 = jnp.where(row > col, second, 0.0).astype(BF16)
    wide = jnp.broadcast_to(second, (HALF, HALF)).astype(BF16)
    whole = dot1(
        jnp.concatenate([jnp.ones((HALF, HALF), BF16), upto], axis=1),
        jnp.concatenate([after1, wide], axis=0),
    )
    return dot1(upto, after1), whole, dot1(upto, after2), row, col


def local_kernel(got_ref, pair_ref, solved_ref):
    gate, beta = columns_of(got_ref)
    keys = got_ref[:, 16:32, :].reshape(TOK, DIM)
    values = got_ref[:, 32:48, :].reshape(TOK, DIM)
    d11, d21, d22, row, col = spans(gate)
    k_col, k_row = row_sums(keys)
    inv_col, inv_row = inv_norm(k_col), inv_norm(k_row)
    strict = row > col
    scale = beta * inv_col
    k1, k2 = keys[:HALF], keys[HALF:]
    l11 = jnp.where(strict, scale[:HALF] * jnp.exp(jnp.where(strict, d11, 0.0)) * dot_t(k1, k1) * inv_row[:, :HALF], 0.0)
    l22 = jnp.where(strict, scale[HALF:] * jnp.exp(jnp.where(strict, d22, 0.0)) * dot_t(k2, k2) * inv_row[:, HALF:], 0.0)
    l21 = scale[HALF:] * jnp.exp(d21) * dot_t(k2, k1) * inv_row[:, :HALF]
    cumul = jnp.concatenate([d11[:, :1], d21[:, :1]], axis=0) + gate[:1]
    gate_wide = jnp.broadcast_to(gate, (TOK, DIM)).astype(BF16)
    later = (row < col).astype(F32).astype(BF16)
    beyond = jnp.concatenate(
        [
            dot1(jnp.concatenate([later, jnp.ones((HALF, HALF), BF16)], axis=1), gate_wide),
            dot1(later, gate_wide[HALF:]),
        ],
        axis=0,
    )
    right = jnp.concatenate(
        [(scale * jnp.exp(cumul)) * keys.astype(F32), beta * values.astype(F32)], axis=1
    )
    apart = iota((DIM, DIM), 0) ^ iota((DIM, DIM), 1)
    eye = jnp.where(apart == 0, 1.0, 0.0)
    blocks = [l11[:DIM, :DIM], l11[DIM:, DIM:], l22[:DIM, :DIM], l22[DIM:, DIM:]]
    n1 = [jnp.where(apart < 16, -b, 0.0) for b in blocks]
    n2 = [dot_pair(n, n) for n in n1]
    x = [eye + n + m + dot_pair(n, m) for n, m in zip(n1, n2)]
    n4 = [dot_pair(n, n) for n in n2]
    x = [y + dot_pair(y, n) for y, n in zip(x, n4)]
    n8 = [dot_pair(n, n) for n in n4]
    x = [y + dot_pair(y, n) for y, n in zip(x, n8)]
    for width in (16, 32, 64):
        here = (apart >= width) & (apart < 2 * width)
        half = [dot_pair(jnp.where(here, b, 0.0), y) for b, y in zip(blocks, x)]
        x = [y - dot_pair(y, z) for y, z in zip(x, half)]
    merged = []
    for lo, hi, tie in ((x[0], x[1], l11[DIM:, :DIM]), (x[2], x[3], l22[DIM:, :DIM])):
        cross = -dot_pair(hi, dot_pair(tie, lo))
        merged.append(
            jnp.concatenate(
                [jnp.concatenate([lo, jnp.zeros_like(lo)], axis=1), jnp.concatenate([cross, hi], axis=1)], axis=0
            )
        )
    top = dot3(merged[0], right[:HALF])
    parts = [top, dot3(merged[1], right[HALF:] - dot3(l21, top))]
    solved = jnp.concatenate(parts, axis=0)
    solved_ref[...] = solved
    weight = inv_col * jnp.exp(beyond)
    scaled = jnp.concatenate([weight, weight], axis=1) * solved
    high, low = split(scaled)
    keys_t = keys.T
    moved = dot1(keys_t, high) + dot1(keys_t, low)
    carry = jnp.where(apart == 0, jnp.exp(cumul[TOK - 1 :]), 0.0)
    pair_ref[:, :DIM] = carry - moved[:, :DIM]
    pair_ref[:, DIM:] = moved[:, DIM:]


def readout_kernel(got_ref, solved_ref, before_ref, direct_ref, reach_ref):
    gate, _ = columns_of(got_ref)
    queries = got_ref[:, 0:16, :].reshape(TOK, DIM)
    keys = got_ref[:, 16:32, :].reshape(TOK, DIM)
    d11, d21, d22, row, col = spans(gate)
    q_col, _ = row_sums(queries)
    _, k_row = row_sums(keys)
    query_inv, key_inv = inv_norm(q_col), inv_norm(k_row)
    inclusive = row >= col
    q1, q2, k1, k2 = queries[:HALF], queries[HALF:], keys[:HALF], keys[HALF:]
    i1, i2 = query_inv[:HALF], query_inv[HALF:]
    s11 = jnp.where(inclusive, i1 * jnp.exp(jnp.where(inclusive, d11, 0.0)) * dot_t(q1, k1) * key_inv[:, :HALF], 0.0)
    s22 = jnp.where(inclusive, i2 * jnp.exp(jnp.where(inclusive, d22, 0.0)) * dot_t(q2, k2) * key_inv[:, HALF:], 0.0)
    s21 = i2 * jnp.exp(d21) * dot_t(q2, k1) * key_inv[:, :HALF]
    cumul = jnp.concatenate([d11[:, :1], d21[:, :1]], axis=0) + gate[:1]
    solved = solved_ref[...]
    top = dot3(s11, solved[:HALF])
    bottom = dot3(jnp.concatenate([s21, s22], axis=1), solved)
    mixed = jnp.concatenate([top, bottom], axis=0)
    reach = query_inv * jnp.exp(cumul) * queries.astype(F32) - mixed[:, :DIM]
    step = dot3(reach, before_ref[...])
    reach_ref[...] = step[:, :DIM]
    direct_ref[...] = mixed[:, DIM:] + step[:, DIM:]


def after(later, earlier):
    step = dot3(later[:, :DIM], earlier)
    return jnp.concatenate([step[:, :DIM], step[:, DIM:] + later[:, DIM:]], axis=1)


def group_kernel(spot_ref, group_ref, before_ref, upto_ref, total_ref):
    spot = spot_ref[0]
    d_row, d_col = iota((DIM, 2 * DIM), 0), iota((DIM, 2 * DIM), 1)
    chain = [jnp.where(d_row == d_col, 1.0, 0.0), group_ref[0]]
    for step in range(1, 4):
        chain.append(after(group_ref[step], chain[-1]))
    before, upto = chain[0], chain[1]
    for step in range(1, 4):
        before = jnp.where(spot == step, chain[step], before)
        upto = jnp.where(spot == step, chain[step + 1], upto)
    before_ref[...] = before
    upto_ref[...] = upto
    total_ref[...] = chain[4]


def last_kernel(one_ref, two_ref, three_ref, upto_ref, direct_ref, reach_ref, out_ref, state_ref):
    arriving = dot3(two_ref[:, :DIM], three_ref[...]) + two_ref[:, DIM:]
    arriving = dot3(one_ref[:, :DIM], arriving) + one_ref[:, DIM:]
    out_ref[...] = (direct_ref[...] + dot3(reach_ref[...], arriving)).astype(BF16)
    state_ref[...] = dot3(upto_ref[:, :DIM], arriving) + upto_ref[:, DIM:]


def call(kernel, *shapes):
    def run(*operands):
        vmem = pl.BlockSpec(memory_space=pltpu.VMEM)
        outs = tuple(jax.ShapeDtypeStruct(shape, dtype) for shape, dtype in shapes)
        return pl.pallas_call(
            kernel,
            out_shape=outs,
            in_specs=[
                pl.BlockSpec(memory_space=pltpu.SMEM) if x.dtype == jnp.int32 else vmem for x in operands
            ],
            out_specs=tuple([vmem] * len(outs)),
            compiler_params=pltpu.CompilerParams(vmem_limit_bytes=48 << 20),
        )(*operands)

    return run


def shifted(block, distance):
    count = lax.axis_size("seq")
    return lax.ppermute(block, "seq", [(i - distance, i) for i in range(distance, count)])


def per_device(query_heads, key_heads, value_heads, gate_log, beta_rate):
    grouping = value_heads.shape[1] // query_heads.shape[1]
    queries = jnp.repeat(jnp.swapaxes(query_heads, 0, 1), grouping, axis=0)
    keys = jnp.repeat(jnp.swapaxes(key_heads, 0, 1), grouping, axis=0)
    values = jnp.swapaxes(value_heads, 0, 1)
    rates = jnp.concatenate([gate_log.T, beta_rate.T], axis=1)[:, None, :]
    rates = jnp.pad(rates, ((0, 0), (0, 7), (0, DIM - 2 * PER)))
    packed = jnp.concatenate([queries, keys, values, rates], axis=1)
    got = lax.all_to_all(packed, "head", split_axis=0, concat_axis=0, tiled=True)
    pair = ((DIM, 2 * DIM), F32)
    own, solved = call(local_kernel, pair, ((TOK, 2 * DIM), F32))(got)
    count = lax.axis_size("seq")
    groups = [list(range(first, first + 4)) for first in range(0, count, 4)]
    group = lax.all_gather(own, "seq", axis_index_groups=groups)
    spot = (lax.axis_index("seq") % 4).astype(jnp.int32)[None]
    before, upto, total = call(group_kernel, pair, pair, pair)(spot, group)
    one, two, three = shifted(total, 4), shifted(total, 8), shifted(total[:, DIM:], 12)
    direct, reach = call(readout_kernel, ((TOK, DIM), F32), ((TOK, DIM), F32))(got, solved, before)
    rows, last_state = call(last_kernel, ((TOK, DIM), BF16), ((DIM, DIM), F32))(
        one, two, three, upto, direct, reach
    )
    head_output = lax.all_to_all(rows, "head", split_axis=0, concat_axis=1, tiled=True)
    return head_output, last_state[None, None]


def solution(mesh):
    return jax.shard_map(
        per_device,
        mesh=mesh,
        in_specs=(
            P(("seq", "head"), None, None),
            P(("seq", "head"), None, None),
            P(("seq", "head"), None, None),
            P(("seq", "head"), None),
            P(("seq", "head"), None),
        ),
        out_specs=(P(("seq", "head"), None), P("seq", "head", None, None)),
        check_vma=False,
    )
```

```python
import jax
import jax.numpy as jnp
from jax import lax
from jax.experimental import pallas as pl
from jax.experimental.pallas import tpu as pltpu
from jax.sharding import PartitionSpec as P

F32 = jnp.float32
BF16 = jnp.bfloat16
TOK = 512
DIM = 128
SRC = 32
PER = 16
HALF = 256


def iota(shape, dim):
    return lax.broadcasted_iota(jnp.int32, shape, dim)


def dot1(a, b):
    return lax.dot_general(a, b, (((1,), (0,)), ((), ())), preferred_element_type=F32)


def dot_t(a, b):
    return lax.dot_general(a, b, (((1,), (1,)), ((), ())), preferred_element_type=F32)


def split(a):
    high = a.astype(BF16)
    return high, (a - high.astype(F32)).astype(BF16)


def dot3(a, b):
    ah, al = split(a)
    bh, bl = split(b)
    return dot1(ah, bh) + (dot1(ah, bl) + dot1(al, bh))


def inv_norm(total):
    total = total + 1e-6
    y = lax.rsqrt(total)
    return y * (1.5 - 0.5 * total * y * y)


def row_sums(x):
    squares = x.astype(F32) * x.astype(F32)
    column = jnp.sum(squares, axis=1, keepdims=True)
    high, low = split(squares)
    ones = jnp.ones((8, DIM), BF16)
    row = (dot_t(ones, high) + dot_t(ones, low))[0:1]
    return column, row


def pack_kernel(*refs):
    packed_ref, sems = refs[5], refs[11]
    copies = [pltpu.make_async_copy(refs[n], refs[6 + n], sems.at[n]) for n in range(5)]
    for copy in copies:
        copy.start()
    for n in range(2):
        copies[n].wait()
        turned = jnp.swapaxes(refs[6 + n][...].astype(F32), 0, 1)
        doubled = jnp.broadcast_to(turned[:, None], (PER, 2, PER, DIM)).reshape(SRC, PER, DIM)
        packed_ref[:, 16 * n : 16 * n + 16, :] = doubled.astype(BF16)
    copies[2].wait()
    packed_ref[:, 32:48, :] = jnp.swapaxes(refs[8][...].astype(F32), 0, 1).astype(BF16)
    copies[3].wait()
    copies[4].wait()
    row, col = iota((PER, DIM), 0), iota((PER, DIM), 1)
    contract = (((0,), (0,)), ((), ()))
    lanes = lax.dot_general(
        refs[9][...], (row == col).astype(F32).astype(BF16), contract, preferred_element_type=F32
    ) + lax.dot_general(
        refs[10][...], (row + PER == col).astype(F32).astype(BF16), contract, preferred_element_type=F32
    )
    packed_ref[:, 48:56, :] = jnp.broadcast_to(lanes[:, None, :], (SRC, 8, DIM)).astype(BF16)


def pack(*operands):
    return pl.pallas_call(
        pack_kernel,
        out_shape=jax.ShapeDtypeStruct((SRC, 56, DIM), BF16),
        in_specs=[pl.BlockSpec(memory_space=pl.ANY)] * 5,
        out_specs=pl.BlockSpec(memory_space=pltpu.VMEM),
        scratch_shapes=[pltpu.VMEM(x.shape, x.dtype) for x in operands] + [pltpu.SemaphoreType.DMA((5,))],
    )(*operands)


def dot_pair(a, b):
    ah, al = split(a)
    bh, bl = split(b)
    return dot1(jnp.concatenate([ah, al], axis=1), jnp.concatenate([bh, bh], axis=0)) + dot1(ah, bl)


def columns_of(got_ref):
    lanes = got_ref[:, 48:56, :].astype(F32)[:, 0, :].astype(BF16)
    token, source = iota((TOK, SRC), 0), iota((TOK, SRC), 1)
    spread = ((token >> 4) == source).astype(F32).astype(BF16)
    rows = dot1(spread, lanes)
    lane = iota((TOK, DIM), 1)
    spot = iota((TOK, DIM), 0) & (PER - 1)
    gate = jnp.sum(jnp.where(lane == spot, rows, 0.0), axis=1, keepdims=True)
    beta = jnp.sum(jnp.where(lane == spot + PER, rows, 0.0), axis=1, keepdims=True)
    return gate, beta


def spans(gate):
    row, col = iota((HALF, HALF), 0), iota((HALF, HALF), 1)
    upto = (row >= col).astype(F32).astype(BF16)
    first, second = gate[:HALF], gate[HALF:]
    after1 = jnp.where(row > col, first, 0.0).astype(BF16)
    after2 = jnp.where(row > col, second, 0.0).astype(BF16)
    wide = jnp.broadcast_to(second, (HALF, HALF)).astype(BF16)
    whole = dot1(
        jnp.concatenate([jnp.ones((HALF, HALF), BF16), upto], axis=1),
        jnp.concatenate([after1, wide], axis=0),
    )
    return dot1(upto, after1), whole, dot1(upto, after2), row, col


def local_kernel(got_ref, pair_ref, solved_ref):
    gate, beta = columns_of(got_ref)
    keys = got_ref[:, 16:32, :].reshape(TOK, DIM)
    values = got_ref[:, 32:48, :].reshape(TOK, DIM)
    d11, d21, d22, row, col = spans(gate)
    k_col, k_row = row_sums(keys)
    inv_col, inv_row = inv_norm(k_col), inv_norm(k_row)
    strict = row > col
    scale = beta * inv_col
    k1, k2 = keys[:HALF], keys[HALF:]
    l11 = jnp.where(strict, scale[:HALF] * jnp.exp(jnp.where(strict, d11, 0.0)) * dot_t(k1, k1) * inv_row[:, :HALF], 0.0)
    l22 = jnp.where(strict, scale[HALF:] * jnp.exp(jnp.where(strict, d22, 0.0)) * dot_t(k2, k2) * inv_row[:, HALF:], 0.0)
    l21 = scale[HALF:] * jnp.exp(d21) * dot_t(k2, k1) * inv_row[:, :HALF]
    cumul = jnp.concatenate([d11[:, :1], d21[:, :1]], axis=0) + gate[:1]
    gate_wide = jnp.broadcast_to(gate, (TOK, DIM)).astype(BF16)
    later = (row < col).astype(F32).astype(BF16)
    beyond = jnp.concatenate(
        [
            dot1(jnp.concatenate([later, jnp.ones((HALF, HALF), BF16)], axis=1), gate_wide),
            dot1(later, gate_wide[HALF:]),
        ],
        axis=0,
    )
    right = jnp.concatenate(
        [(scale * jnp.exp(cumul)) * keys.astype(F32), beta * values.astype(F32)], axis=1
    )
    apart = iota((DIM, DIM), 0) ^ iota((DIM, DIM), 1)
    eye = jnp.where(apart == 0, 1.0, 0.0)
    blocks = [l11[:DIM, :DIM], l11[DIM:, DIM:], l22[:DIM, :DIM], l22[DIM:, DIM:]]
    n1 = [jnp.where(apart < 16, -b, 0.0) for b in blocks]
    n2 = [dot_pair(n, n) for n in n1]
    x = [eye + n + m + dot_pair(n, m) for n, m in zip(n1, n2)]
    n4 = [dot_pair(n, n) for n in n2]
    x = [y + dot_pair(y, n) for y, n in zip(x, n4)]
    n8 = [dot_pair(n, n) for n in n4]
    x = [y + dot_pair(y, n) for y, n in zip(x, n8)]
    for width in (16, 32, 64):
        here = (apart >= width) & (apart < 2 * width)
        half = [dot_pair(jnp.where(here, b, 0.0), y) for b, y in zip(blocks, x)]
        x = [y - dot_pair(y, z) for y, z in zip(x, half)]
    merged = []
    for lo, hi, tie in ((x[0], x[1], l11[DIM:, :DIM]), (x[2], x[3], l22[DIM:, :DIM])):
        cross = -dot_pair(hi, dot_pair(tie, lo))
        merged.append(
            jnp.concatenate(
                [jnp.concatenate([lo, jnp.zeros_like(lo)], axis=1), jnp.concatenate([cross, hi], axis=1)], axis=0
            )
        )
    top = dot3(merged[0], right[:HALF])
    parts = [top, dot3(merged[1], right[HALF:] - dot3(l21, top))]
    solved = jnp.concatenate(parts, axis=0)
    solved_ref[...] = solved
    weight = inv_col * jnp.exp(beyond)
    scaled = jnp.concatenate([weight, weight], axis=1) * solved
    high, low = split(scaled)
    keys_t = keys.T
    moved = dot1(keys_t, high) + dot1(keys_t, low)
    carry = jnp.where(apart == 0, jnp.exp(cumul[TOK - 1 :]), 0.0)
    pair_ref[:, :DIM] = carry - moved[:, :DIM]
    pair_ref[:, DIM:] = moved[:, DIM:]


def readout_kernel(got_ref, solved_ref, before_ref, direct_ref, reach_ref):
    gate, _ = columns_of(got_ref)
    queries = got_ref[:, 0:16, :].reshape(TOK, DIM)
    keys = got_ref[:, 16:32, :].reshape(TOK, DIM)
    d11, d21, d22, row, col = spans(gate)
    q_col, _ = row_sums(queries)
    _, k_row = row_sums(keys)
    query_inv, key_inv = inv_norm(q_col), inv_norm(k_row)
    inclusive = row >= col
    q1, q2, k1, k2 = queries[:HALF], queries[HALF:], keys[:HALF], keys[HALF:]
    i1, i2 = query_inv[:HALF], query_inv[HALF:]
    s11 = jnp.where(inclusive, i1 * jnp.exp(jnp.where(inclusive, d11, 0.0)) * dot_t(q1, k1) * key_inv[:, :HALF], 0.0)
    s22 = jnp.where(inclusive, i2 * jnp.exp(jnp.where(inclusive, d22, 0.0)) * dot_t(q2, k2) * key_inv[:, HALF:], 0.0)
    s21 = i2 * jnp.exp(d21) * dot_t(q2, k1) * key_inv[:, :HALF]
    cumul = jnp.concatenate([d11[:, :1], d21[:, :1]], axis=0) + gate[:1]
    solved = solved_ref[...]
    top = dot3(s11, solved[:HALF])
    bottom = dot3(jnp.concatenate([s21, s22], axis=1), solved)
    mixed = jnp.concatenate([top, bottom], axis=0)
    reach = query_inv * jnp.exp(cumul) * queries.astype(F32) - mixed[:, :DIM]
    step = dot3(reach, before_ref[...])
    reach_ref[...] = step[:, :DIM]
    direct_ref[...] = mixed[:, DIM:] + step[:, DIM:]


def after(later, earlier):
    step = dot_pair(later[:, :DIM], earlier)
    return jnp.concatenate([step[:, :DIM], step[:, DIM:] + later[:, DIM:]], axis=1)


def group_kernel(spot_ref, group_ref, before_ref, upto_ref, total_ref):
    spot = spot_ref[0]
    d_row, d_col = iota((DIM, 2 * DIM), 0), iota((DIM, 2 * DIM), 1)
    first = group_ref[0]
    two = after(group_ref[1], first)
    late = after(group_ref[3], group_ref[2])
    chain = [jnp.where(d_row == d_col, 1.0, 0.0), first, two, after(group_ref[2], two), after(late, two)]
    before, upto = chain[0], chain[1]
    for step in range(1, 4):
        before = jnp.where(spot == step, chain[step], before)
        upto = jnp.where(spot == step, chain[step + 1], upto)
    before_ref[...] = before
    upto_ref[...] = upto
    total_ref[...] = chain[4]


def last_kernel(near_ref, three_ref, upto_ref, direct_ref, reach_ref, out_ref, state_ref):
    arriving = dot_pair(near_ref[1, :, :DIM], three_ref[...]) + near_ref[1, :, DIM:]
    arriving = dot_pair(near_ref[0, :, :DIM], arriving) + near_ref[0, :, DIM:]
    state_ref[...] = dot_pair(upto_ref[:, :DIM], arriving) + upto_ref[:, DIM:]
    out_ref[...] = (direct_ref[...] + dot_pair(reach_ref[...], arriving)).astype(BF16)


def call(kernel, *shapes):
    def run(*operands):
        vmem = pl.BlockSpec(memory_space=pltpu.VMEM)
        outs = tuple(jax.ShapeDtypeStruct(shape, dtype) for shape, dtype in shapes)
        return pl.pallas_call(
            kernel,
            out_shape=outs,
            in_specs=[
                pl.BlockSpec(memory_space=pltpu.SMEM) if x.dtype == jnp.int32 else vmem for x in operands
            ],
            out_specs=tuple([vmem] * len(outs)),
            compiler_params=pltpu.CompilerParams(vmem_limit_bytes=48 << 20),
        )(*operands)

    return run


def shifted(block, distance):
    count = lax.axis_size("seq")
    return lax.ppermute(block, "seq", [(i - distance, i) for i in range(distance, count)])


def per_device(query_heads, key_heads, value_heads, gate_log, beta_rate):
    packed = pack(query_heads, key_heads, value_heads, gate_log, beta_rate)
    got = lax.all_to_all(packed, "head", split_axis=0, concat_axis=0, tiled=True)
    pair = ((DIM, 2 * DIM), F32)
    own, solved = call(local_kernel, pair, ((TOK, 2 * DIM), F32))(got)
    count = lax.axis_size("seq")
    groups = [list(range(first, first + 4)) for first in range(0, count, 4)]
    group = lax.all_gather(own, "seq", axis_index_groups=groups)
    spot = (lax.axis_index("seq") % 4).astype(jnp.int32)[None]
    before, upto, total = call(group_kernel, pair, pair, pair)(spot, group)
    route = [(i - 4 * (1 + i % 2), i) for i in range(count) if i >= 4 * (1 + i % 2)]
    mixed = lax.ppermute(total, "seq", route)
    three = shifted(total[:, DIM:], 12)
    direct, reach = call(readout_kernel, ((TOK, DIM), F32), ((TOK, DIM), F32))(got, solved, before)
    near = lax.all_gather(mixed, "seq", axis_index_groups=[[i, i + 1] for i in range(0, count, 2)])
    rows, last_state = call(last_kernel, ((TOK, DIM), BF16), ((DIM, DIM), F32))(
        near, three, upto, direct, reach
    )
    head_output = lax.all_to_all(rows, "head", split_axis=0, concat_axis=1, tiled=True)
    return head_output, last_state[None, None]


def solution(mesh):
    return jax.shard_map(
        per_device,
        mesh=mesh,
        in_specs=(
            P(("seq", "head"), None, None),
            P(("seq", "head"), None, None),
            P(("seq", "head"), None, None),
            P(("seq", "head"), None),
            P(("seq", "head"), None),
        ),
        out_specs=(P(("seq", "head"), None), P("seq", "head", None, None)),
        check_vma=False,
    )
```

```python
import jax
import jax.numpy as jnp
from jax import lax
from jax.experimental import pallas as pl
from jax.experimental.pallas import tpu as pltpu
from jax.sharding import PartitionSpec as P

F32 = jnp.float32
BF16 = jnp.bfloat16
TOK = 512
DIM = 128
SRC = 32
PER = 16
HALF = 256


def iota(shape, dim):
    return lax.broadcasted_iota(jnp.int32, shape, dim)


def dot1(a, b):
    return lax.dot_general(a, b, (((1,), (0,)), ((), ())), preferred_element_type=F32)


def dot_t(a, b):
    return lax.dot_general(a, b, (((1,), (1,)), ((), ())), preferred_element_type=F32)


def split(a):
    high = a.astype(BF16)
    return high, (a - high.astype(F32)).astype(BF16)


def dot3(a, b):
    ah, al = split(a)
    bh, bl = split(b)
    return dot1(ah, bh) + (dot1(ah, bl) + dot1(al, bh))


def inv_norm(total):
    total = total + 1e-6
    y = lax.rsqrt(total)
    return y * (1.5 - 0.5 * total * y * y)


def row_sums(x):
    squares = x.astype(F32) * x.astype(F32)
    column = jnp.sum(squares, axis=1, keepdims=True)
    high, low = split(squares)
    ones = jnp.ones((8, DIM), BF16)
    row = (dot_t(ones, high) + dot_t(ones, low))[0:1]
    return column, row


def column_sums(x):
    wide = x.astype(F32)
    return jnp.sum(wide * wide, axis=1, keepdims=True)


def diagonal(square, row, col):
    return jnp.sum(jnp.where(row == col, square, 0.0), axis=0, keepdims=True)


def pack_kernel(*refs):
    packed_ref, sems = refs[5], refs[11]
    copies = [pltpu.make_async_copy(refs[n], refs[6 + n], sems.at[n]) for n in range(5)]
    for copy in copies:
        copy.start()
    for n in range(2):
        copies[n].wait()
        turned = jnp.swapaxes(refs[6 + n][...].astype(F32), 0, 1).astype(BF16).reshape(PER, 8, 2, DIM)
        packed_ref[:, 8 * n : 8 * n + 8] = jnp.broadcast_to(turned[:, None], (PER, 2, 8, 2, DIM)).reshape(SRC, 8, 2, DIM)
    copies[2].wait()
    packed_ref[:, 16:24] = jnp.swapaxes(refs[8][...].astype(F32), 0, 1).astype(BF16).reshape(SRC, 8, 2, DIM)
    copies[3].wait()
    copies[4].wait()
    row, col = iota((PER, DIM), 0), iota((PER, DIM), 1)
    contract = (((0,), (0,)), ((), ()))
    lanes = lax.dot_general(
        refs[9][...], (row == col).astype(F32).astype(BF16), contract, preferred_element_type=F32
    ) + lax.dot_general(
        refs[10][...], (row + PER == col).astype(F32).astype(BF16), contract, preferred_element_type=F32
    )
    packed_ref[:, 24] = jnp.broadcast_to(lanes[:, None, :], (SRC, 2, DIM)).astype(BF16)


def pack(*operands):
    return pl.pallas_call(
        pack_kernel,
        out_shape=jax.ShapeDtypeStruct((SRC, 25, 2, DIM), BF16),
        in_specs=[pl.BlockSpec(memory_space=pl.ANY)] * 5,
        out_specs=pl.BlockSpec(memory_space=pltpu.VMEM),
        scratch_shapes=[pltpu.VMEM(x.shape, x.dtype) for x in operands] + [pltpu.SemaphoreType.DMA((5,))],
    )(*operands)


def dot_pair(a, b):
    ah, al = split(a)
    bh, bl = split(b)
    return dot1(jnp.concatenate([ah, al], axis=1), jnp.concatenate([bh, bh], axis=0)) + dot1(ah, bl)


def columns_of(got_ref):
    lanes = got_ref[:, 24].astype(F32)[:, 0, :].astype(BF16)
    token, source = iota((TOK, SRC), 0), iota((TOK, SRC), 1)
    spread = ((token >> 4) == source).astype(F32).astype(BF16)
    rows = dot1(spread, lanes)
    lane = iota((TOK, DIM), 1)
    spot = iota((TOK, DIM), 0) & (PER - 1)
    gate = jnp.sum(jnp.where(lane == spot, rows, 0.0), axis=1, keepdims=True)
    beta = jnp.sum(jnp.where(lane == spot + PER, rows, 0.0), axis=1, keepdims=True)
    return gate, beta


def spans(gate):
    row, col = iota((HALF, HALF), 0), iota((HALF, HALF), 1)
    upto = (row >= col).astype(F32).astype(BF16)
    first, second = gate[:HALF], gate[HALF:]
    after1 = jnp.where(row > col, first, 0.0).astype(BF16)
    after2 = jnp.where(row > col, second, 0.0).astype(BF16)
    wide = jnp.broadcast_to(second, (HALF, HALF)).astype(BF16)
    whole = dot1(
        jnp.concatenate([jnp.ones((HALF, HALF), BF16), upto], axis=1),
        jnp.concatenate([after1, wide], axis=0),
    )
    return dot1(upto, after1), whole, dot1(upto, after2), row, col


def picked(x, width):
    return jnp.concatenate([x[at : at + width] for at in range(width, DIM, 2 * width)], axis=0)


def spread_out(x, width):
    gap = jnp.zeros((width, x.shape[1]), x.dtype)
    return jnp.concatenate([y for at in range(0, DIM // 2, width) for y in (gap, x[at : at + width])], axis=0)


def local_kernel(got_ref, pair_ref, solved_ref):
    gate, beta = columns_of(got_ref)
    keys = got_ref[:, 8:16].reshape(TOK, DIM)
    values = got_ref[:, 16:24].reshape(TOK, DIM)
    d11, d21, d22, row, col = spans(gate)
    inv_col = inv_norm(column_sums(keys))
    strict = row > col
    scale = beta * inv_col
    k1, k2 = keys[:HALF], keys[HALF:]
    kk1, kk2 = dot_t(k1, k1), dot_t(k2, k2)
    inv1, inv2 = inv_norm(diagonal(kk1, row, col)), inv_norm(diagonal(kk2, row, col))
    l11 = jnp.where(strict, scale[:HALF] * jnp.exp(jnp.where(strict, d11, 0.0)) * kk1 * inv1, 0.0)
    l22 = jnp.where(strict, scale[HALF:] * jnp.exp(jnp.where(strict, d22, 0.0)) * kk2 * inv2, 0.0)
    l21 = scale[HALF:] * jnp.exp(d21) * dot_t(k2, k1) * inv1
    cumul = jnp.concatenate([d11[:, :1], d21[:, :1]], axis=0) + gate[:1]
    gate_wide = jnp.broadcast_to(gate, (TOK, DIM)).astype(BF16)
    later = (row < col).astype(F32).astype(BF16)
    beyond = jnp.concatenate(
        [
            dot1(jnp.concatenate([later, jnp.ones((HALF, HALF), BF16)], axis=1), gate_wide),
            dot1(later, gate_wide[HALF:]),
        ],
        axis=0,
    )
    right = jnp.concatenate(
        [(scale * jnp.exp(cumul)) * keys.astype(F32), beta * values.astype(F32)], axis=1
    )
    apart = iota((DIM, DIM), 0) ^ iota((DIM, DIM), 1)
    eye = jnp.where(apart == 0, 1.0, 0.0)
    blocks = [l11[:DIM, :DIM], l11[DIM:, DIM:], l22[:DIM, :DIM], l22[DIM:, DIM:]]
    n1 = [jnp.where(apart < 16, -b, 0.0) for b in blocks]
    n2 = [dot_pair(n, n) for n in n1]
    x = [eye + n + m + dot_pair(n, m) for n, m in zip(n1, n2)]
    n4 = [dot_pair(n, n) for n in n2]
    x = [y + dot_pair(y, n) for y, n in zip(x, n4)]
    n8 = [dot_pair(n, n) for n in n4]
    x = [y + dot_pair(y, n) for y, n in zip(x, n8)]
    for width in (16, 32, 64):
        here = picked(apart, width)
        here = (here >= width) & (here < 2 * width)
        half = [dot_pair(jnp.where(here, picked(b, width), 0.0), y) for b, y in zip(blocks, x)]
        step = [dot_pair(picked(y, width), spread_out(z, width)) for y, z in zip(x, half)]
        x = [y - spread_out(z, width) for y, z in zip(x, step)]
    merged = []
    for lo, hi, tie in ((x[0], x[1], l11[DIM:, :DIM]), (x[2], x[3], l22[DIM:, :DIM])):
        cross = -dot_pair(hi, dot_pair(tie, lo))
        merged.append(
            jnp.concatenate(
                [jnp.concatenate([lo, jnp.zeros_like(lo)], axis=1), jnp.concatenate([cross, hi], axis=1)], axis=0
            )
        )
    top = dot3(merged[0], right[:HALF])
    parts = [top, dot3(merged[1], right[HALF:] - dot3(l21, top))]
    solved = jnp.concatenate(parts, axis=0)
    solved_ref[...] = solved
    weight = inv_col * jnp.exp(beyond)
    scaled = jnp.concatenate([weight, weight], axis=1) * solved
    high, low = split(scaled)
    keys_t = keys.T
    moved = dot1(keys_t, high) + dot1(keys_t, low)
    carry = jnp.where(apart == 0, jnp.exp(cumul[TOK - 1 :]), 0.0)
    pair_ref[:, :DIM] = carry - moved[:, :DIM]
    pair_ref[:, DIM:] = moved[:, DIM:]


def readout_kernel(got_ref, solved_ref, before_ref, direct_ref, reach_ref):
    gate, _ = columns_of(got_ref)
    queries = got_ref[:, 0:8].reshape(TOK, DIM)
    keys = got_ref[:, 8:16].reshape(TOK, DIM)
    d11, d21, d22, row, col = spans(gate)
    q_col, _ = row_sums(queries)
    _, k_row = row_sums(keys)
    query_inv, key_inv = inv_norm(q_col), inv_norm(k_row)
    inclusive = row >= col
    q1, q2, k1, k2 = queries[:HALF], queries[HALF:], keys[:HALF], keys[HALF:]
    i1, i2 = query_inv[:HALF], query_inv[HALF:]
    s11 = jnp.where(inclusive, i1 * jnp.exp(jnp.where(inclusive, d11, 0.0)) * dot_t(q1, k1) * key_inv[:, :HALF], 0.0)
    s22 = jnp.where(inclusive, i2 * jnp.exp(jnp.where(inclusive, d22, 0.0)) * dot_t(q2, k2) * key_inv[:, HALF:], 0.0)
    s21 = i2 * jnp.exp(d21) * dot_t(q2, k1) * key_inv[:, :HALF]
    cumul = jnp.concatenate([d11[:, :1], d21[:, :1]], axis=0) + gate[:1]
    solved = solved_ref[...]
    top = dot3(s11, solved[:HALF])
    bottom = dot3(jnp.concatenate([s21, s22], axis=1), solved)
    mixed = jnp.concatenate([top, bottom], axis=0)
    reach = query_inv * jnp.exp(cumul) * queries.astype(F32) - mixed[:, :DIM]
    step = dot3(reach, before_ref[...])
    reach_ref[...] = step[:, :DIM]
    direct_ref[...] = mixed[:, DIM:] + step[:, DIM:]


def after(later, earlier):
    step = dot_pair(later[:, :DIM], earlier)
    return jnp.concatenate([step[:, :DIM], step[:, DIM:] + later[:, DIM:]], axis=1)


def group_kernel(spot_ref, group_ref, before_ref, upto_ref, total_ref):
    spot = spot_ref[0]
    d_row, d_col = iota((DIM, 2 * DIM), 0), iota((DIM, 2 * DIM), 1)
    first = group_ref[0]
    two = after(group_ref[1], first)
    late = after(group_ref[3], group_ref[2])
    chain = [jnp.where(d_row == d_col, 1.0, 0.0), first, two, after(group_ref[2], two), after(late, two)]
    before, upto = chain[0], chain[1]
    for step in range(1, 4):
        before = jnp.where(spot == step, chain[step], before)
        upto = jnp.where(spot == step, chain[step + 1], upto)
    before_ref[...] = before
    upto_ref[...] = upto
    total_ref[...] = chain[4]


def last_kernel(near_ref, three_ref, upto_ref, direct_ref, reach_ref, out_ref, state_ref):
    arriving = dot_pair(near_ref[1, :, :DIM], three_ref[...]) + near_ref[1, :, DIM:]
    arriving = dot_pair(near_ref[0, :, :DIM], arriving) + near_ref[0, :, DIM:]
    state_ref[...] = dot_pair(upto_ref[:, :DIM], arriving) + upto_ref[:, DIM:]
    out_ref[...] = (direct_ref[...] + dot_pair(reach_ref[...], arriving)).astype(BF16)


def call(kernel, *shapes):
    def run(*operands):
        vmem = pl.BlockSpec(memory_space=pltpu.VMEM)
        outs = tuple(jax.ShapeDtypeStruct(shape, dtype) for shape, dtype in shapes)
        return pl.pallas_call(
            kernel,
            out_shape=outs,
            in_specs=[
                pl.BlockSpec(memory_space=pltpu.SMEM) if x.dtype == jnp.int32 else vmem for x in operands
            ],
            out_specs=tuple([vmem] * len(outs)),
            compiler_params=pltpu.CompilerParams(vmem_limit_bytes=48 << 20),
        )(*operands)

    return run


def shifted(block, distance):
    count = lax.axis_size("seq")
    return lax.ppermute(block, "seq", [(i - distance, i) for i in range(distance, count)])


def per_device(query_heads, key_heads, value_heads, gate_log, beta_rate):
    packed = pack(query_heads, key_heads, value_heads, gate_log, beta_rate)
    got = lax.all_to_all(packed, "head", split_axis=0, concat_axis=0, tiled=True)
    pair = ((DIM, 2 * DIM), F32)
    own, solved = call(local_kernel, pair, ((TOK, 2 * DIM), F32))(got)
    count = lax.axis_size("seq")
    groups = [list(range(first, first + 4)) for first in range(0, count, 4)]
    group = lax.all_gather(own, "seq", axis_index_groups=groups)
    spot = (lax.axis_index("seq") % 4).astype(jnp.int32)[None]
    before, upto, total = call(group_kernel, pair, pair, pair)(spot, group)
    route = [(i - 4 * (1 + i % 2), i) for i in range(count) if i >= 4 * (1 + i % 2)]
    mixed = lax.ppermute(total, "seq", route)
    three = shifted(total[:, DIM:], 12)
    direct, reach = call(readout_kernel, ((TOK, DIM), F32), ((TOK, DIM), F32))(got, solved, before)
    near = lax.all_gather(mixed, "seq", axis_index_groups=[[i, i + 1] for i in range(0, count, 2)])
    rows, last_state = call(last_kernel, ((TOK, DIM), BF16), ((DIM, DIM), F32))(
        near, three, upto, direct, reach
    )
    head_output = lax.all_to_all(rows, "head", split_axis=0, concat_axis=1, tiled=True)
    return head_output, last_state[None, None]


def solution(mesh):
    return jax.shard_map(
        per_device,
        mesh=mesh,
        in_specs=(
            P(("seq", "head"), None, None),
            P(("seq", "head"), None, None),
            P(("seq", "head"), None, None),
            P(("seq", "head"), None),
            P(("seq", "head"), None),
        ),
        out_specs=(P(("seq", "head"), None), P("seq", "head", None, None)),
        check_vma=False,
    )
```

```python
import jax
import jax.numpy as jnp
from jax import lax
from jax.experimental import pallas as pl
from jax.experimental.pallas import tpu as pltpu
from jax.sharding import PartitionSpec as P

F32 = jnp.float32
BF16 = jnp.bfloat16
TOK = 512
DIM = 128
SRC = 32
PER = 16
HALF = 256


def iota(shape, dim):
    return lax.broadcasted_iota(jnp.int32, shape, dim)


def dot1(a, b):
    return lax.dot_general(a, b, (((1,), (0,)), ((), ())), preferred_element_type=F32)


def dot_t(a, b):
    return lax.dot_general(a, b, (((1,), (1,)), ((), ())), preferred_element_type=F32)


def split(a):
    high = a.astype(BF16)
    return high, (a - high.astype(F32)).astype(BF16)


def dot3(a, b):
    ah, al = split(a)
    bh, bl = split(b)
    return dot1(ah, bh) + (dot1(ah, bl) + dot1(al, bh))


def inv_norm(total):
    total = total + 1e-6
    y = lax.rsqrt(total)
    return y * (1.5 - 0.5 * total * y * y)


def row_sums(x):
    squares = x.astype(F32) * x.astype(F32)
    column = jnp.sum(squares, axis=1, keepdims=True)
    high, low = split(squares)
    ones = jnp.ones((8, DIM), BF16)
    row = (dot_t(ones, high) + dot_t(ones, low))[0:1]
    return column, row


def column_sums(x):
    wide = x.astype(F32)
    return jnp.sum(wide * wide, axis=1, keepdims=True)


def diagonal(square, row, col):
    return jnp.sum(jnp.where(row == col, square, 0.0), axis=0, keepdims=True)


def pack_kernel(*refs):
    packed_ref, ins, parts, sems, gone = refs[5], refs[6:11], refs[11:15], refs[15], refs[16]
    copies = [pltpu.make_async_copy(refs[n], ins[n], sems.at[n]) for n in range(5)]
    sent = [
        pltpu.make_async_copy(part, packed_ref.at[:, 8 * n : 8 * n + part.shape[1]], gone.at[n])
        for n, part in enumerate(parts)
    ]
    for n in (3, 4, 2, 0, 1):
        copies[n].start()
    copies[3].wait()
    copies[4].wait()
    row, col = iota((PER, DIM), 0), iota((PER, DIM), 1)
    contract = (((0,), (0,)), ((), ()))
    lanes = lax.dot_general(
        ins[3][...], (row == col).astype(F32).astype(BF16), contract, preferred_element_type=F32
    ) + lax.dot_general(
        ins[4][...], (row + PER == col).astype(F32).astype(BF16), contract, preferred_element_type=F32
    )
    parts[3][:, 0] = jnp.broadcast_to(lanes[:, None, :], (SRC, 2, DIM)).astype(BF16)
    sent[3].start()
    copies[2].wait()
    parts[2][...] = jnp.swapaxes(ins[2][...].astype(F32), 0, 1).astype(BF16).reshape(SRC, 8, 2, DIM)
    sent[2].start()
    for n in range(2):
        copies[n].wait()
        turned = jnp.swapaxes(ins[n][...].astype(F32), 0, 1).astype(BF16).reshape(PER, 8, 2, DIM)
        parts[n][...] = jnp.broadcast_to(turned[:, None], (PER, 2, 8, 2, DIM)).reshape(SRC, 8, 2, DIM)
        sent[n].start()
    for copy in sent:
        copy.wait()


def pack(*operands):
    hbm = pl.BlockSpec(memory_space=pl.ANY)
    return pl.pallas_call(
        pack_kernel,
        out_shape=jax.ShapeDtypeStruct((SRC, 25, 2, DIM), BF16),
        in_specs=[hbm] * 5,
        out_specs=hbm,
        scratch_shapes=[pltpu.VMEM(x.shape, x.dtype) for x in operands]
        + [pltpu.VMEM((SRC, n, 2, DIM), BF16) for n in (8, 8, 8, 1)]
        + [pltpu.SemaphoreType.DMA((5,)), pltpu.SemaphoreType.DMA((4,))],
    )(*operands)


def dot_pair(a, b):
    ah, al = split(a)
    bh, bl = split(b)
    return dot1(jnp.concatenate([ah, al], axis=1), jnp.concatenate([bh, bh], axis=0)) + dot1(ah, bl)


def columns_of(got_ref):
    lanes = got_ref[:, 24].astype(F32)[:, 0, :].astype(BF16)
    token, source = iota((TOK, SRC), 0), iota((TOK, SRC), 1)
    spread = ((token >> 4) == source).astype(F32).astype(BF16)
    rows = dot1(spread, lanes)
    lane = iota((TOK, DIM), 1)
    spot = iota((TOK, DIM), 0) & (PER - 1)
    gate = jnp.sum(jnp.where(lane == spot, rows, 0.0), axis=1, keepdims=True)
    beta = jnp.sum(jnp.where(lane == spot + PER, rows, 0.0), axis=1, keepdims=True)
    return gate, beta


def chunks(x):
    return [x[at : at + DIM] for at in range(0, TOK, DIM)]


def spans(gate):
    row, col = iota((DIM, DIM), 0), iota((DIM, DIM), 1)
    upto = (row >= col).astype(F32).astype(BF16)
    steps = chunks(gate)
    after_all = jnp.concatenate([jnp.where(row > col, g, 0.0).astype(BF16) for g in steps], axis=1)
    wide = dot1(upto, after_all)
    differ = [wide[:, at : at + DIM] for at in range(0, TOK, DIM)]
    return differ, [d[:, :1] + g[:1] for d, g in zip(differ, steps)], row, col


def picked(x, width):
    return jnp.concatenate([x[at : at + width] for at in range(width, DIM, 2 * width)], axis=0)


def spread_out(x, width):
    gap = jnp.zeros((width, x.shape[1]), x.dtype)
    return jnp.concatenate([y for at in range(0, DIM // 2, width) for y in (gap, x[at : at + width])], axis=0)


def after(later, earlier):
    step = dot_pair(later[:, :DIM], earlier)
    return jnp.concatenate([step[:, :DIM], step[:, DIM:] + later[:, DIM:]], axis=1)


def local_kernel(got_ref, pair_ref, solved_ref, maps_ref):
    gate, beta = columns_of(got_ref)
    keys = got_ref[:, 8:16].reshape(TOK, DIM)
    values = got_ref[:, 16:24].reshape(TOK, DIM)
    differ, cumul, row, col = spans(gate)
    key_inv = inv_norm(column_sums(keys))
    strict = row > col
    later = (row < col).astype(F32).astype(BF16)
    gates = jnp.concatenate([jnp.broadcast_to(g, (DIM, DIM)).astype(BF16) for g in chunks(gate)], axis=1)
    beyond = dot1(later, gates)
    keys, values, scale, beta, key_inv = (chunks(x) for x in (keys, values, beta * key_inv, beta, key_inv))
    blocks, right = [], []
    for k, v, d, c, sc, b in zip(keys, values, differ, cumul, scale, beta):
        key_key = dot_t(k, k)
        inv_row = inv_norm(diagonal(key_key, row, col))
        blocks.append(jnp.where(strict, sc * jnp.exp(jnp.where(strict, d, 0.0)) * key_key * inv_row, 0.0))
        right.append(jnp.concatenate([(sc * jnp.exp(c)) * k.astype(F32), b * v.astype(F32)], axis=1))
    apart = row ^ col
    eye = jnp.where(apart == 0, 1.0, 0.0)
    n1 = [jnp.where(apart < 16, -b, 0.0) for b in blocks]
    n2 = [dot_pair(n, n) for n in n1]
    x = [eye + n + m + dot_pair(n, m) for n, m in zip(n1, n2)]
    n4 = [dot_pair(n, n) for n in n2]
    x = [y + dot_pair(y, n) for y, n in zip(x, n4)]
    n8 = [dot_pair(n, n) for n in n4]
    x = [y + dot_pair(y, n) for y, n in zip(x, n8)]
    for width in (16, 32, 64):
        here = picked(apart, width)
        here = (here >= width) & (here < 2 * width)
        half = [dot_pair(jnp.where(here, picked(b, width), 0.0), y) for b, y in zip(blocks, x)]
        step = [dot_pair(picked(y, width), spread_out(z, width)) for y, z in zip(x, half)]
        x = [y - spread_out(z, width) for y, z in zip(x, step)]
    maps = []
    for at in range(4):
        solved = dot_pair(x[at], right[at])
        solved_ref[DIM * at : DIM * at + DIM, :] = solved
        weight = key_inv[at] * jnp.exp(beyond[:, DIM * at : DIM * at + DIM])
        high, low = split(jnp.concatenate([weight, weight], axis=1) * solved)
        keys_t = keys[at].T
        moved = dot1(jnp.concatenate([keys_t, keys_t], axis=1), jnp.concatenate([high, low], axis=0))
        kept = jnp.where(apart == 0, jnp.exp(cumul[at][DIM - 1 :]), 0.0)
        maps.append(jnp.concatenate([kept - moved[:, :DIM], moved[:, DIM:]], axis=1))
    early, late = after(maps[1], maps[0]), after(maps[3], maps[2])
    pair_ref[...] = after(late, early)
    maps_ref[0] = maps[0]
    maps_ref[1] = early
    maps_ref[2] = maps[2]


def readout_kernel(got_ref, solved_ref, maps_ref, before_ref, direct_ref, reach_ref):
    gate, _ = columns_of(got_ref)
    queries = got_ref[:, 0:8].reshape(TOK, DIM)
    keys = got_ref[:, 8:16].reshape(TOK, DIM)
    differ, cumul, row, col = spans(gate)
    query_inv = chunks(inv_norm(column_sums(queries)))
    inclusive = row >= col
    first = before_ref[...]
    half = after(maps_ref[1], first)
    starts = [first, after(maps_ref[0], first), half, after(maps_ref[2], half)]
    for at, (q, k, d, c, i, start) in enumerate(zip(chunks(queries), chunks(keys), differ, cumul, query_inv, starts)):
        key_inv = inv_norm(diagonal(dot_t(k, k), row, col))
        scores = jnp.where(inclusive, i * jnp.exp(jnp.where(inclusive, d, 0.0)) * dot_t(q, k) * key_inv, 0.0)
        span = slice(DIM * at, DIM * at + DIM)
        mixed = dot_pair(scores, solved_ref[span, :])
        step = dot_pair(i * jnp.exp(c) * q.astype(F32) - mixed[:, :DIM], start)
        reach_ref[span, :] = step[:, :DIM]
        direct_ref[span, :] = mixed[:, DIM:] + step[:, DIM:]


def group_kernel(spot_ref, group_ref, before_ref, upto_ref, total_ref):
    spot = spot_ref[0]
    d_row, d_col = iota((DIM, 2 * DIM), 0), iota((DIM, 2 * DIM), 1)
    first = group_ref[0]
    two = after(group_ref[1], first)
    late = after(group_ref[3], group_ref[2])
    chain = [jnp.where(d_row == d_col, 1.0, 0.0), first, two, after(group_ref[2], two), after(late, two)]
    before, upto = chain[0], chain[1]
    for step in range(1, 4):
        before = jnp.where(spot == step, chain[step], before)
        upto = jnp.where(spot == step, chain[step + 1], upto)
    before_ref[...] = before
    upto_ref[...] = upto
    total_ref[...] = chain[4]


def last_kernel(near_ref, three_ref, upto_ref, direct_ref, reach_ref, out_ref, state_ref):
    arriving = dot_pair(near_ref[1, :, :DIM], three_ref[...]) + near_ref[1, :, DIM:]
    arriving = dot_pair(near_ref[0, :, :DIM], arriving) + near_ref[0, :, DIM:]
    state_ref[...] = dot_pair(upto_ref[:, :DIM], arriving) + upto_ref[:, DIM:]
    out_ref[...] = (direct_ref[...] + dot_pair(reach_ref[...], arriving)).astype(BF16)


def call(kernel, *shapes):
    def run(*operands):
        vmem = pl.BlockSpec(memory_space=pltpu.VMEM)
        outs = tuple(jax.ShapeDtypeStruct(shape, dtype) for shape, dtype in shapes)
        return pl.pallas_call(
            kernel,
            out_shape=outs,
            in_specs=[
                pl.BlockSpec(memory_space=pltpu.SMEM) if x.dtype == jnp.int32 else vmem for x in operands
            ],
            out_specs=tuple([vmem] * len(outs)),
            compiler_params=pltpu.CompilerParams(vmem_limit_bytes=48 << 20),
        )(*operands)

    return run


def shifted(block, distance):
    count = lax.axis_size("seq")
    return lax.ppermute(block, "seq", [(i - distance, i) for i in range(distance, count)])


def per_device(query_heads, key_heads, value_heads, gate_log, beta_rate):
    packed = pack(query_heads, key_heads, value_heads, gate_log, beta_rate)
    got = lax.all_to_all(packed, "head", split_axis=0, concat_axis=0, tiled=True)
    pair = ((DIM, 2 * DIM), F32)
    own, solved, maps = call(local_kernel, pair, ((TOK, 2 * DIM), F32), ((3, DIM, 2 * DIM), F32))(got)
    count = lax.axis_size("seq")
    groups = [list(range(first, first + 4)) for first in range(0, count, 4)]
    group = lax.all_gather(own, "seq", axis_index_groups=groups)
    spot = (lax.axis_index("seq") % 4).astype(jnp.int32)[None]
    before, upto, total = call(group_kernel, pair, pair, pair)(spot, group)
    route = [(i - 4 * (1 + i % 2), i) for i in range(count) if i >= 4 * (1 + i % 2)]
    mixed = lax.ppermute(total, "seq", route)
    three = shifted(total[:, DIM:], 12)
    direct, reach = call(readout_kernel, ((TOK, DIM), F32), ((TOK, DIM), F32))(got, solved, maps, before)
    near = lax.all_gather(mixed, "seq", axis_index_groups=[[i, i + 1] for i in range(0, count, 2)])
    rows, last_state = call(last_kernel, ((TOK, DIM), BF16), ((DIM, DIM), F32))(
        near, three, upto, direct, reach
    )
    head_output = lax.all_to_all(rows, "head", split_axis=0, concat_axis=1, tiled=True)
    return head_output, last_state[None, None]


def solution(mesh):
    return jax.shard_map(
        per_device,
        mesh=mesh,
        in_specs=(
            P(("seq", "head"), None, None),
            P(("seq", "head"), None, None),
            P(("seq", "head"), None, None),
            P(("seq", "head"), None),
            P(("seq", "head"), None),
        ),
        out_specs=(P(("seq", "head"), None), P("seq", "head", None, None)),
        check_vma=False,
    )
```

```python
import jax
import jax.numpy as jnp
from jax import lax
from jax.experimental import pallas as pl
from jax.experimental.pallas import tpu as pltpu
from jax.sharding import PartitionSpec as P

F32 = jnp.float32
BF16 = jnp.bfloat16
TOK = 512
DIM = 128
SRC = 32
PER = 16
HALF = 256


def iota(shape, dim):
    return lax.broadcasted_iota(jnp.int32, shape, dim)


def dot1(a, b):
    return lax.dot_general(a, b, (((1,), (0,)), ((), ())), preferred_element_type=F32)


def dot_t(a, b):
    return lax.dot_general(a, b, (((1,), (1,)), ((), ())), preferred_element_type=F32)


def split(a):
    high = a.astype(BF16)
    return high, (a - high.astype(F32)).astype(BF16)


def dot3(a, b):
    ah, al = split(a)
    bh, bl = split(b)
    return dot1(ah, bh) + (dot1(ah, bl) + dot1(al, bh))


def inv_norm(total):
    total = total + 1e-6
    y = lax.rsqrt(total)
    return y * (1.5 - 0.5 * total * y * y)


def row_sums(x):
    squares = x.astype(F32) * x.astype(F32)
    column = jnp.sum(squares, axis=1, keepdims=True)
    high, low = split(squares)
    ones = jnp.ones((8, DIM), BF16)
    row = (dot_t(ones, high) + dot_t(ones, low))[0:1]
    return column, row


def column_sums(x):
    wide = x.astype(F32)
    return jnp.sum(wide * wide, axis=1, keepdims=True)


def diagonal(square, row, col):
    return jnp.sum(jnp.where(row == col, square, 0.0), axis=0, keepdims=True)


def pack_kernel(*refs):
    packed_ref, ins, parts, sems, gone = refs[5], refs[6:11], refs[11:15], refs[15], refs[16]
    copies = [pltpu.make_async_copy(refs[n], ins[n], sems.at[n]) for n in range(5)]
    sent = [
        pltpu.make_async_copy(part, packed_ref.at[:, 8 * n : 8 * n + part.shape[1]], gone.at[n])
        for n, part in enumerate(parts)
    ]
    for n in (3, 4, 2, 0, 1):
        copies[n].start()
    copies[3].wait()
    copies[4].wait()
    row, col = iota((PER, DIM), 0), iota((PER, DIM), 1)
    contract = (((0,), (0,)), ((), ()))
    lanes = lax.dot_general(
        ins[3][...], (row == col).astype(F32).astype(BF16), contract, preferred_element_type=F32
    ) + lax.dot_general(
        ins[4][...], (row + PER == col).astype(F32).astype(BF16), contract, preferred_element_type=F32
    )
    parts[3][:, 0] = jnp.broadcast_to(lanes[:, None, :], (SRC, 2, DIM)).astype(BF16)
    sent[3].start()
    copies[2].wait()
    parts[2][...] = jnp.swapaxes(ins[2][...].astype(F32), 0, 1).astype(BF16).reshape(SRC, 8, 2, DIM)
    sent[2].start()
    for n in range(2):
        copies[n].wait()
        turned = jnp.swapaxes(ins[n][...].astype(F32), 0, 1).astype(BF16).reshape(PER, 8, 2, DIM)
        parts[n][...] = jnp.broadcast_to(turned[:, None], (PER, 2, 8, 2, DIM)).reshape(SRC, 8, 2, DIM)
        sent[n].start()
    for copy in sent:
        copy.wait()


def pack(*operands):
    hbm = pl.BlockSpec(memory_space=pl.ANY)
    return pl.pallas_call(
        pack_kernel,
        out_shape=jax.ShapeDtypeStruct((SRC, 25, 2, DIM), BF16),
        in_specs=[hbm] * 5,
        out_specs=hbm,
        scratch_shapes=[pltpu.VMEM(x.shape, x.dtype) for x in operands]
        + [pltpu.VMEM((SRC, n, 2, DIM), BF16) for n in (8, 8, 8, 1)]
        + [pltpu.SemaphoreType.DMA((5,)), pltpu.SemaphoreType.DMA((4,))],
    )(*operands)


def dot_pair(a, b):
    ah, al = split(a)
    bh, bl = split(b)
    return dot1(jnp.concatenate([ah, al], axis=1), jnp.concatenate([bh, bh], axis=0)) + dot1(ah, bl)


def columns_of(got_ref):
    lanes = got_ref[:, 24].astype(F32)[:, 0, :].astype(BF16)
    token, source = iota((TOK, SRC), 0), iota((TOK, SRC), 1)
    spread = ((token >> 4) == source).astype(F32).astype(BF16)
    rows = dot1(spread, lanes)
    lane = iota((TOK, DIM), 1)
    spot = iota((TOK, DIM), 0) & (PER - 1)
    gate = jnp.sum(jnp.where(lane == spot, rows, 0.0), axis=1, keepdims=True)
    beta = jnp.sum(jnp.where(lane == spot + PER, rows, 0.0), axis=1, keepdims=True)
    return gate, beta


def chunks(x):
    return [x[at : at + DIM] for at in range(0, TOK, DIM)]


def spans(gate):
    row, col = iota((DIM, DIM), 0), iota((DIM, DIM), 1)
    upto = (row >= col).astype(F32).astype(BF16)
    steps = chunks(gate)
    after_all = jnp.concatenate([jnp.where(row > col, g, 0.0).astype(BF16) for g in steps], axis=1)
    wide = dot1(upto, after_all)
    differ = [wide[:, at : at + DIM] for at in range(0, TOK, DIM)]
    return differ, [d[:, :1] + g[:1] for d, g in zip(differ, steps)], row, col


def picked(x, width):
    return jnp.concatenate([x[at : at + width] for at in range(width, DIM, 2 * width)], axis=0)


def spread_out(x, width):
    gap = jnp.zeros((width, x.shape[1]), x.dtype)
    return jnp.concatenate([y for at in range(0, DIM // 2, width) for y in (gap, x[at : at + width])], axis=0)


def after(later, earlier):
    step = dot_pair(later[:, :DIM], earlier)
    return jnp.concatenate([step[:, :DIM], step[:, DIM:] + later[:, DIM:]], axis=1)


def local_kernel(got_ref, pair_ref, solved_ref, maps_ref):
    gate, beta = columns_of(got_ref)
    keys = got_ref[:, 8:16].reshape(TOK, DIM)
    values = got_ref[:, 16:24].reshape(TOK, DIM)
    differ, cumul, row, col = spans(gate)
    key_inv = inv_norm(column_sums(keys))
    strict = row > col
    later = (row < col).astype(F32).astype(BF16)
    gates = jnp.concatenate([jnp.broadcast_to(g, (DIM, DIM)).astype(BF16) for g in chunks(gate)], axis=1)
    beyond = dot1(later, gates)
    keys, values, scale, beta, key_inv = (chunks(x) for x in (keys, values, beta * key_inv, beta, key_inv))
    blocks, right = [], []
    for k, v, d, c, sc, b in zip(keys, values, differ, cumul, scale, beta):
        key_key = dot_t(k, k)
        inv_row = inv_norm(diagonal(key_key, row, col))
        blocks.append(jnp.where(strict, sc * jnp.exp(jnp.where(strict, d, 0.0)) * key_key * inv_row, 0.0))
        right.append(jnp.concatenate([(sc * jnp.exp(c)) * k.astype(F32), b * v.astype(F32)], axis=1))
    apart = row ^ col
    eye = jnp.where(apart == 0, 1.0, 0.0)
    n1 = [jnp.where(apart < 16, -b, 0.0) for b in blocks]
    n2 = [dot_pair(n, n) for n in n1]
    both = [dot_pair(jnp.concatenate([n, m], axis=0), m) for n, m in zip(n1, n2)]
    x = [eye + n + m + t[:DIM] for n, m, t in zip(n1, n2, both)]
    n4 = [t[DIM:] for t in both]
    both = [dot_pair(jnp.concatenate([y, n], axis=0), n) for y, n in zip(x, n4)]
    x = [y + t[:DIM] for y, t in zip(x, both)]
    x = [y + dot_pair(y, t[DIM:]) for y, t in zip(x, both)]
    for width in (16, 32, 64):
        here = picked(apart, width)
        here = (here >= width) & (here < 2 * width)
        half = [dot_pair(jnp.where(here, picked(b, width), 0.0), y) for b, y in zip(blocks, x)]
        step = [dot_pair(picked(y, width), spread_out(z, width)) for y, z in zip(x, half)]
        x = [y - spread_out(z, width) for y, z in zip(x, step)]
    maps = []
    for at in range(4):
        solved = dot_pair(x[at], right[at])
        solved_ref[DIM * at : DIM * at + DIM, :] = solved
        weight = key_inv[at] * jnp.exp(beyond[:, DIM * at : DIM * at + DIM])
        high, low = split(jnp.concatenate([weight, weight], axis=1) * solved)
        keys_t = keys[at].T
        moved = dot1(jnp.concatenate([keys_t, keys_t], axis=1), jnp.concatenate([high, low], axis=0))
        kept = jnp.where(apart == 0, jnp.exp(cumul[at][DIM - 1 :]), 0.0)
        maps.append(jnp.concatenate([kept - moved[:, :DIM], moved[:, DIM:]], axis=1))
    early, late = after(maps[1], maps[0]), after(maps[3], maps[2])
    pair_ref[...] = after(late, early)
    maps_ref[0] = maps[0]
    maps_ref[1] = early
    maps_ref[2] = maps[2]


def readout_kernel(got_ref, solved_ref, maps_ref, before_ref, direct_ref, reach_ref):
    gate, _ = columns_of(got_ref)
    queries = got_ref[:, 0:8].reshape(TOK, DIM)
    keys = got_ref[:, 8:16].reshape(TOK, DIM)
    differ, cumul, row, col = spans(gate)
    query_inv = chunks(inv_norm(column_sums(queries)))
    inclusive = row >= col
    first = before_ref[...]
    half = after(maps_ref[1], first)
    starts = [first, after(maps_ref[0], first), half, after(maps_ref[2], half)]
    for at, (q, k, d, c, i, start) in enumerate(zip(chunks(queries), chunks(keys), differ, cumul, query_inv, starts)):
        key_inv = inv_norm(diagonal(dot_t(k, k), row, col))
        scores = jnp.where(inclusive, i * jnp.exp(jnp.where(inclusive, d, 0.0)) * dot_t(q, k) * key_inv, 0.0)
        span = slice(DIM * at, DIM * at + DIM)
        mixed = dot_pair(scores, solved_ref[span, :])
        step = dot_pair(i * jnp.exp(c) * q.astype(F32) - mixed[:, :DIM], start)
        reach_ref[span, :] = step[:, :DIM]
        direct_ref[span, :] = mixed[:, DIM:] + step[:, DIM:]


def group_kernel(group_ref, before_ref, upto_ref, total_ref):
    spot = lax.axis_index("seq") % 4
    d_row, d_col = iota((DIM, 2 * DIM), 0), iota((DIM, 2 * DIM), 1)
    first = group_ref[0]
    two = after(group_ref[1], first)
    late = after(group_ref[3], group_ref[2])
    chain = [jnp.where(d_row == d_col, 1.0, 0.0), first, two, after(group_ref[2], two), after(late, two)]
    before, upto = chain[0], chain[1]
    for step in range(1, 4):
        before = jnp.where(spot == step, chain[step], before)
        upto = jnp.where(spot == step, chain[step + 1], upto)
    before_ref[...] = before
    upto_ref[...] = upto
    total_ref[...] = chain[4]


def last_kernel(near_ref, three_ref, upto_ref, direct_ref, reach_ref, out_ref, state_ref):
    arriving = dot_pair(near_ref[1, :, :DIM], three_ref[...]) + near_ref[1, :, DIM:]
    arriving = dot_pair(near_ref[0, :, :DIM], arriving) + near_ref[0, :, DIM:]
    state_ref[...] = dot_pair(upto_ref[:, :DIM], arriving) + upto_ref[:, DIM:]
    out_ref[...] = (direct_ref[...] + dot_pair(reach_ref[...], arriving)).astype(BF16)


def call(kernel, *shapes):
    def run(*operands):
        vmem = pl.BlockSpec(memory_space=pltpu.VMEM)
        outs = tuple(jax.ShapeDtypeStruct(shape, dtype) for shape, dtype in shapes)
        return pl.pallas_call(
            kernel,
            out_shape=outs,
            in_specs=[
                pl.BlockSpec(memory_space=pltpu.SMEM) if x.dtype == jnp.int32 else vmem for x in operands
            ],
            out_specs=tuple([vmem] * len(outs)),
            compiler_params=pltpu.CompilerParams(vmem_limit_bytes=48 << 20),
        )(*operands)

    return run


def shifted(block, distance):
    count = lax.axis_size("seq")
    return lax.ppermute(block, "seq", [(i - distance, i) for i in range(distance, count)])


def per_device(query_heads, key_heads, value_heads, gate_log, beta_rate):
    packed = pack(query_heads, key_heads, value_heads, gate_log, beta_rate)
    got = lax.all_to_all(packed, "head", split_axis=0, concat_axis=0, tiled=True)
    pair = ((DIM, 2 * DIM), F32)
    own, solved, maps = call(local_kernel, pair, ((TOK, 2 * DIM), F32), ((3, DIM, 2 * DIM), F32))(got)
    count = lax.axis_size("seq")
    groups = [list(range(first, first + 4)) for first in range(0, count, 4)]
    group = lax.all_gather(own, "seq", axis_index_groups=groups)
    before, upto, total = call(group_kernel, pair, pair, pair)(group)
    route = [(i - 4 * (1 + i % 2), i) for i in range(count) if i >= 4 * (1 + i % 2)]
    mixed = lax.ppermute(total, "seq", route)
    three = shifted(total[:, DIM:], 12)
    direct, reach = call(readout_kernel, ((TOK, DIM), F32), ((TOK, DIM), F32))(got, solved, maps, before)
    near = lax.all_gather(mixed, "seq", axis_index_groups=[[i, i + 1] for i in range(0, count, 2)])
    rows, last_state = call(last_kernel, ((TOK, DIM), BF16), ((DIM, DIM), F32))(
        near, three, upto, direct, reach
    )
    head_output = lax.all_to_all(rows, "head", split_axis=0, concat_axis=1, tiled=True)
    return head_output, last_state[None, None]


def solution(mesh):
    return jax.shard_map(
        per_device,
        mesh=mesh,
        in_specs=(
            P(("seq", "head"), None, None),
            P(("seq", "head"), None, None),
            P(("seq", "head"), None, None),
            P(("seq", "head"), None),
            P(("seq", "head"), None),
        ),
        out_specs=(P(("seq", "head"), None), P("seq", "head", None, None)),
        check_vma=False,
    )
```

```python
import jax
import jax.numpy as jnp
from jax import lax
from jax.experimental import pallas as pl
from jax.experimental.pallas import tpu as pltpu
from jax.sharding import PartitionSpec as P

F32 = jnp.float32
BF16 = jnp.bfloat16
TOK = 512
DIM = 128
SRC = 32
PER = 16
HALF = 256


def iota(shape, dim):
    return lax.broadcasted_iota(jnp.int32, shape, dim)


def dot1(a, b):
    return lax.dot_general(a, b, (((1,), (0,)), ((), ())), preferred_element_type=F32)


def dot_t(a, b):
    return lax.dot_general(a, b, (((1,), (1,)), ((), ())), preferred_element_type=F32)


def split(a):
    high = a.astype(BF16)
    return high, (a - high.astype(F32)).astype(BF16)


def dot3(a, b):
    ah, al = split(a)
    bh, bl = split(b)
    return dot1(ah, bh) + (dot1(ah, bl) + dot1(al, bh))


def inv_norm(total):
    total = total + 1e-6
    y = lax.rsqrt(total)
    return y * (1.5 - 0.5 * total * y * y)


def row_sums(x):
    squares = x.astype(F32) * x.astype(F32)
    column = jnp.sum(squares, axis=1, keepdims=True)
    high, low = split(squares)
    ones = jnp.ones((8, DIM), BF16)
    row = (dot_t(ones, high) + dot_t(ones, low))[0:1]
    return column, row


def column_sums(x):
    wide = x.astype(F32)
    return jnp.sum(wide * wide, axis=1, keepdims=True)


def diagonal(square, row, col):
    return jnp.sum(jnp.where(row == col, square, 0.0), axis=0, keepdims=True)


def pack_kernel(*refs):
    packed_ref, ins, parts, sems, gone = refs[5], refs[6:11], refs[11:15], refs[15], refs[16]
    copies = [pltpu.make_async_copy(refs[n], ins[n], sems.at[n]) for n in range(5)]
    sent = [
        pltpu.make_async_copy(part, packed_ref.at[:, 8 * n : 8 * n + part.shape[1]], gone.at[n])
        for n, part in enumerate(parts)
    ]
    for n in (3, 4, 2, 0, 1):
        copies[n].start()
    copies[3].wait()
    copies[4].wait()
    row, col = iota((PER, DIM), 0), iota((PER, DIM), 1)
    contract = (((0,), (0,)), ((), ()))
    lanes = lax.dot_general(
        ins[3][...], (row == col).astype(F32).astype(BF16), contract, preferred_element_type=F32
    ) + lax.dot_general(
        ins[4][...], (row + PER == col).astype(F32).astype(BF16), contract, preferred_element_type=F32
    )
    parts[3][:, 0] = jnp.broadcast_to(lanes[:, None, :], (SRC, 2, DIM)).astype(BF16)
    sent[3].start()
    copies[2].wait()
    parts[2][...] = jnp.swapaxes(ins[2][...].astype(F32), 0, 1).astype(BF16).reshape(SRC, 8, 2, DIM)
    sent[2].start()
    for n in range(2):
        copies[n].wait()
        turned = jnp.swapaxes(ins[n][...].astype(F32), 0, 1).astype(BF16).reshape(PER, 8, 2, DIM)
        parts[n][...] = jnp.broadcast_to(turned[:, None], (PER, 2, 8, 2, DIM)).reshape(SRC, 8, 2, DIM)
        sent[n].start()
    for copy in sent:
        copy.wait()


def pack(*operands):
    hbm = pl.BlockSpec(memory_space=pl.ANY)
    return pl.pallas_call(
        pack_kernel,
        out_shape=jax.ShapeDtypeStruct((SRC, 25, 2, DIM), BF16),
        in_specs=[hbm] * 5,
        out_specs=hbm,
        scratch_shapes=[pltpu.VMEM(x.shape, x.dtype) for x in operands]
        + [pltpu.VMEM((SRC, n, 2, DIM), BF16) for n in (8, 8, 8, 1)]
        + [pltpu.SemaphoreType.DMA((5,)), pltpu.SemaphoreType.DMA((4,))],
    )(*operands)


def dot_pair(a, b):
    ah, al = split(a)
    bh, bl = split(b)
    return dot1(jnp.concatenate([ah, al], axis=1), jnp.concatenate([bh, bh], axis=0)) + dot1(ah, bl)


def columns_of(got_ref):
    lanes = got_ref[:, 24].astype(F32)[:, 0, :].astype(BF16)
    token, source = iota((TOK, SRC), 0), iota((TOK, SRC), 1)
    spread = ((token >> 4) == source).astype(F32).astype(BF16)
    rows = dot1(spread, lanes)
    lane = iota((TOK, DIM), 1)
    spot = iota((TOK, DIM), 0) & (PER - 1)
    gate = jnp.sum(jnp.where(lane == spot, rows, 0.0), axis=1, keepdims=True)
    beta = jnp.sum(jnp.where(lane == spot + PER, rows, 0.0), axis=1, keepdims=True)
    return gate, beta


def chunks(x):
    return [x[at : at + DIM] for at in range(0, TOK, DIM)]


def spans(gate):
    row, col = iota((DIM, DIM), 0), iota((DIM, DIM), 1)
    upto = (row >= col).astype(F32).astype(BF16)
    steps = chunks(gate)
    after_all = jnp.concatenate([jnp.where(row > col, g, 0.0).astype(BF16) for g in steps], axis=1)
    wide = dot1(upto, after_all)
    differ = [wide[:, at : at + DIM] for at in range(0, TOK, DIM)]
    return differ, [d[:, :1] + g[:1] for d, g in zip(differ, steps)], row, col


def picked(x, width):
    return jnp.concatenate([x[at : at + width] for at in range(width, DIM, 2 * width)], axis=0)


def spread_out(x, width):
    gap = jnp.zeros((width, x.shape[1]), x.dtype)
    return jnp.concatenate([y for at in range(0, DIM // 2, width) for y in (gap, x[at : at + width])], axis=0)


def after(later, earlier):
    step = dot_pair(later[:, :DIM], earlier)
    return jnp.concatenate([step[:, :DIM], step[:, DIM:] + later[:, DIM:]], axis=1)


def local_kernel(got_ref, pair_ref, solved_ref, maps_ref):
    gate, beta = columns_of(got_ref)
    keys = got_ref[:, 8:16].reshape(TOK, DIM)
    values = got_ref[:, 16:24].reshape(TOK, DIM)
    differ, cumul, row, col = spans(gate)
    key_inv = inv_norm(column_sums(keys))
    strict = row > col
    later = (row < col).astype(F32).astype(BF16)
    gates = jnp.concatenate([jnp.broadcast_to(g, (DIM, DIM)).astype(BF16) for g in chunks(gate)], axis=1)
    beyond = dot1(later, gates)
    keys, values, scale, beta, key_inv = (chunks(x) for x in (keys, values, beta * key_inv, beta, key_inv))
    blocks, right = [], []
    for k, v, d, c, sc, b in zip(keys, values, differ, cumul, scale, beta):
        key_key = dot_t(k, k)
        inv_row = inv_norm(diagonal(key_key, row, col))
        blocks.append(jnp.where(strict, sc * jnp.exp(jnp.where(strict, d, 0.0)) * key_key * inv_row, 0.0))
        right.append(jnp.concatenate([(sc * jnp.exp(c)) * k.astype(F32), b * v.astype(F32)], axis=1))
    apart = row ^ col
    eye = jnp.where(apart == 0, 1.0, 0.0)
    n1 = [jnp.where(apart < 16, -b, 0.0) for b in blocks]
    n2 = [dot_pair(n, n) for n in n1]
    both = [dot_pair(jnp.concatenate([n, m], axis=0), m) for n, m in zip(n1, n2)]
    x = [eye + n + m + t[:DIM] for n, m, t in zip(n1, n2, both)]
    n4 = [t[DIM:] for t in both]
    both = [dot_pair(jnp.concatenate([y, n], axis=0), n) for y, n in zip(x, n4)]
    x = [y + t[:DIM] for y, t in zip(x, both)]
    x = [y + dot_pair(y, t[DIM:]) for y, t in zip(x, both)]
    for width in (16, 32, 64):
        here = picked(apart, width)
        here = (here >= width) & (here < 2 * width)
        half = [dot_pair(jnp.where(here, picked(b, width), 0.0), y) for b, y in zip(blocks, x)]
        step = [dot_pair(picked(y, width), spread_out(z, width)) for y, z in zip(x, half)]
        x = [y - spread_out(z, width) for y, z in zip(x, step)]
    maps = []
    for at in range(4):
        solved = dot_pair(x[at], right[at])
        solved_ref[DIM * at : DIM * at + DIM, :] = solved
        weight = key_inv[at] * jnp.exp(beyond[:, DIM * at : DIM * at + DIM])
        high, low = split(jnp.concatenate([weight, weight], axis=1) * solved)
        keys_t = keys[at].T
        moved = dot1(jnp.concatenate([keys_t, keys_t], axis=1), jnp.concatenate([high, low], axis=0))
        kept = jnp.where(apart == 0, jnp.exp(cumul[at][DIM - 1 :]), 0.0)
        maps.append(jnp.concatenate([kept - moved[:, :DIM], moved[:, DIM:]], axis=1))
    early, late = after(maps[1], maps[0]), after(maps[3], maps[2])
    pair_ref[...] = after(late, early)
    maps_ref[0] = maps[0]
    maps_ref[1] = early
    maps_ref[2] = maps[2]


def readout_kernel(got_ref, solved_ref, maps_ref, before_ref, direct_ref, reach_ref):
    gate, _ = columns_of(got_ref)
    queries = got_ref[:, 0:8].reshape(TOK, DIM)
    keys = got_ref[:, 8:16].reshape(TOK, DIM)
    differ, cumul, row, col = spans(gate)
    query_inv = chunks(inv_norm(column_sums(queries)))
    inclusive = row >= col
    first = before_ref[...]
    half = after(maps_ref[1], first)
    starts = [first, after(maps_ref[0], first), half, after(maps_ref[2], half)]
    for at, (q, k, d, c, i, start) in enumerate(zip(chunks(queries), chunks(keys), differ, cumul, query_inv, starts)):
        key_inv = inv_norm(diagonal(dot_t(k, k), row, col))
        scores = jnp.where(inclusive, i * jnp.exp(jnp.where(inclusive, d, 0.0)) * dot_t(q, k) * key_inv, 0.0)
        span = slice(DIM * at, DIM * at + DIM)
        mixed = dot_pair(scores, solved_ref[span, :])
        step = dot_pair(i * jnp.exp(c) * q.astype(F32) - mixed[:, :DIM], start)
        reach_ref[span, :] = step[:, :DIM]
        direct_ref[span, :] = mixed[:, DIM:] + step[:, DIM:]


def group_kernel(group_ref, before_ref, upto_ref, total_ref):
    spot = lax.axis_index("seq") % 4
    d_row, d_col = iota((DIM, 2 * DIM), 0), iota((DIM, 2 * DIM), 1)
    first = group_ref[0]
    two = after(group_ref[1], first)
    late = after(group_ref[3], group_ref[2])
    chain = [jnp.where(d_row == d_col, 1.0, 0.0), first, two, after(group_ref[2], two), after(late, two)]
    before, upto = chain[0], chain[1]
    for step in range(1, 4):
        before = jnp.where(spot == step, chain[step], before)
        upto = jnp.where(spot == step, chain[step + 1], upto)
    before_ref[...] = before
    upto_ref[...] = upto
    total_ref[...] = chain[4]


def last_kernel(near_ref, three_ref, upto_ref, direct_ref, reach_ref, out_ref, state_ref, state, sem):
    arriving = dot_pair(near_ref[1, :, :DIM], three_ref[...]) + near_ref[1, :, DIM:]
    arriving = dot_pair(near_ref[0, :, :DIM], arriving) + near_ref[0, :, DIM:]
    state[...] = dot_pair(upto_ref[:, :DIM], arriving) + upto_ref[:, DIM:]
    copy = pltpu.make_async_copy(state, state_ref, sem)
    copy.start()
    out_ref[...] = (direct_ref[...] + dot_pair(reach_ref[...], arriving)).astype(BF16)
    copy.wait()


def finish(*operands):
    vmem = pl.BlockSpec(memory_space=pltpu.VMEM)
    return pl.pallas_call(
        last_kernel,
        out_shape=(jax.ShapeDtypeStruct((TOK, DIM), BF16), jax.ShapeDtypeStruct((DIM, DIM), F32)),
        in_specs=[vmem] * len(operands),
        out_specs=(vmem, pl.BlockSpec(memory_space=pl.ANY)),
        scratch_shapes=[pltpu.VMEM((DIM, DIM), F32), pltpu.SemaphoreType.DMA],
        compiler_params=pltpu.CompilerParams(vmem_limit_bytes=48 << 20),
    )(*operands)


def call(kernel, *shapes):
    def run(*operands):
        vmem = pl.BlockSpec(memory_space=pltpu.VMEM)
        outs = tuple(jax.ShapeDtypeStruct(shape, dtype) for shape, dtype in shapes)
        return pl.pallas_call(
            kernel,
            out_shape=outs,
            in_specs=[
                pl.BlockSpec(memory_space=pltpu.SMEM) if x.dtype == jnp.int32 else vmem for x in operands
            ],
            out_specs=tuple([vmem] * len(outs)),
            compiler_params=pltpu.CompilerParams(vmem_limit_bytes=48 << 20),
        )(*operands)

    return run


def shifted(block, distance):
    count = lax.axis_size("seq")
    return lax.ppermute(block, "seq", [(i - distance, i) for i in range(distance, count)])


def per_device(query_heads, key_heads, value_heads, gate_log, beta_rate):
    packed = pack(query_heads, key_heads, value_heads, gate_log, beta_rate)
    got = lax.all_to_all(packed, "head", split_axis=0, concat_axis=0, tiled=True)
    pair = ((DIM, 2 * DIM), F32)
    own, solved, maps = call(local_kernel, pair, ((TOK, 2 * DIM), F32), ((3, DIM, 2 * DIM), F32))(got)
    count = lax.axis_size("seq")
    groups = [list(range(first, first + 4)) for first in range(0, count, 4)]
    group = lax.all_gather(own, "seq", axis_index_groups=groups)
    before, upto, total = call(group_kernel, pair, pair, pair)(group)
    route = [(i - 4 * (1 + i % 2), i) for i in range(count) if i >= 4 * (1 + i % 2)]
    mixed = lax.ppermute(total, "seq", route)
    three = shifted(total[:, DIM:], 12)
    direct, reach = call(readout_kernel, ((TOK, DIM), F32), ((TOK, DIM), F32))(got, solved, maps, before)
    near = lax.all_gather(mixed, "seq", axis_index_groups=[[i, i + 1] for i in range(0, count, 2)])
    rows, last_state = finish(near, three, upto, direct, reach)
    head_output = lax.all_to_all(rows, "head", split_axis=0, concat_axis=1, tiled=True)
    return head_output, last_state[None, None]


def solution(mesh):
    return jax.shard_map(
        per_device,
        mesh=mesh,
        in_specs=(
            P(("seq", "head"), None, None),
            P(("seq", "head"), None, None),
            P(("seq", "head"), None, None),
            P(("seq", "head"), None),
            P(("seq", "head"), None),
        ),
        out_specs=(P(("seq", "head"), None), P("seq", "head", None, None)),
        check_vma=False,
    )
```
